512 devices in a mesh: pipe: 16 (over z_lo, y), dp: 32 (over z_hi, x, core).
Axes of the slice: x: 4, y: 4, z: 16 (z_hi: 4, z_lo: 4; z = z_hi * 4 + z_lo), core: 2. Of those that a mesh axis runs over, the one named last changes fastest.
Arguments:
- queries: bfloat16 [16, 4096, 4096], P('pipe', 'dp'), may hold values from -6 to 6
- out_grad: bfloat16 [16, 4096, 4096], P('pipe', 'dp'), may hold values from -6 to 6
- keys: bfloat16 [16, 2048, 512], P('pipe', 'dp'), may hold values from -6 to 6
- values: bfloat16 [16, 2048, 512], P('pipe', 'dp'), may hold values from -6 to 6
- kv_weight: bfloat16 [16, 8192, 1024], P('pipe', 'dp'), may hold values from -0.0625 to 0.0625
- stream: bfloat16 [2048, 8192], P(None, 'dp'), may hold values from -640 to 640
- norm_gain: float32 [8192], P('dp'), may hold values from 0.1 to 1.9
- lengths: int32 [32], P('dp'), may hold values from 32 to 128, as said below
Outputs:
- kv_weight_grad: float32 [16, 8192, 1024], P('pipe', 'dp')
- latent_grad: bfloat16 [2048, 8192], P('pipe', 'dp')
- gain_grad: float32 [8192], P('dp')
The draws below stay inside these ranges and needn't reach their ends.
Inputs may be any that keep to these rules, and one draw needn't show every extreme that they name: `lengths`: each micro-batch has 32 to 128 live tokens; some micro-batch has exactly 128 and another exactly 32.
All inputs are finite; a program needn't handle non-finite values.
Results may differ from the reference program's by a relative error of at most 0.0057.
Values may be sent and summed in bfloat16 or wider, within the bound.
A program may use at most 64 MiB of HBM per device.

```python
import math
import jax
import jax.numpy as jnp
from jax import lax

D = 8192
HQ = 32
KVH = 4
HD = 128
LAT = 64
TXT = 128
KVW = 512
SECTIONS = 16
GROUPS = 32


def draw_queries(key, part):
    full_shape = (SECTIONS, GROUPS * TXT, HQ * HD)
    base = jax.random.normal(jax.random.fold_in(key, 1), full_shape, jnp.float32)
    return jnp.clip(base, -6.0, 6.0).astype(jnp.bfloat16)


def draw_keys(key, part):
    full_shape = (SECTIONS, GROUPS * LAT, KVH * HD)
    base = jax.random.normal(jax.random.fold_in(key, 2), full_shape, jnp.float32)
    return jnp.clip(base, -6.0, 6.0).astype(jnp.bfloat16)


def draw_stream(key, part):
    row_total = GROUPS * LAT
    column = jnp.arange(D, dtype=jnp.float32) / D
    jitter = jax.random.uniform(jax.random.fold_in(key, 3), (D,), jnp.float32, 0.6, 1.5)
    row_scale = jnp.power(10.0, jax.random.uniform(jax.random.fold_in(key, 4), (row_total, 1), jnp.float32))
    base = jnp.clip(jax.random.normal(jax.random.fold_in(key, 5), (row_total, D), jnp.float32), -4.0, 4.0)
    col_scale = jnp.power(10.0, column) * jitter
    return jnp.clip(base * row_scale * col_scale[None, :], -640.0, 640.0).astype(jnp.bfloat16)


def draw_lengths(key, part):
    drawn = jax.random.randint(jax.random.fold_in(key, 8), (GROUPS,), TXT // 4, TXT + 1, dtype=jnp.int32)
    full_at = jax.random.randint(jax.random.fold_in(key, 9), (), 0, GROUPS, dtype=jnp.int32)
    offset = jax.random.randint(jax.random.fold_in(key, 10), (), 1, GROUPS, dtype=jnp.int32)
    short_at = (full_at + offset) % GROUPS
    positions = jnp.arange(GROUPS, dtype=jnp.int32)
    drawn = jnp.where(positions == short_at, TXT // 4, drawn)
    drawn = jnp.where(positions == full_at, TXT, drawn)
    return drawn.astype(jnp.int32)


def steps_of(stream_key, dims, cuts, smallest, high):
    def one(position, shards_of):
        draws = jax.random.uniform(jax.random.fold_in(jax.random.fold_in(stream_key, 6), position), (shards_of,), jnp.float32, smallest / len(cuts), high / len(cuts))
        return jnp.repeat(jnp.exp(draws), dims[position] // shards_of).reshape((-1,) + (1,) * (len(dims) - position - 1))

    factor_of = one(*cuts[0])
    for cut in cuts[1:]:
        factor_of = factor_of * one(*cut)
    return factor_of


def bell_draw(stream_key, extent, deviation, limit, split=(), kind=jnp.bfloat16):
    entries = jax.random.normal(stream_key, extent, jnp.float32) * deviation
    if len(split) > 0:
        entries = steps_of(stream_key, extent, split, -0.22, 0.18) * entries
    return jnp.clip(entries, min=-limit, max=limit).astype(kind)


def setup_inputs(seed: int = 0) -> dict:
    key_of = jax.random.split(jax.random.key(seed), 9)
    return {
        "queries": draw_queries(jax.random.fold_in(key_of[8], 71), 0),
        "out_grad": bell_draw(key_of[1], (SECTIONS, GROUPS * TXT, HQ * HD), 1.0, 6.0, ((0, 16), (1, 32))),
        "keys": draw_keys(jax.random.fold_in(key_of[8], 71), 0),
        "values": bell_draw(key_of[3], (SECTIONS, GROUPS * LAT, KVW), 1.0, 6.0, ((0, 16), (1, 32))),
        "kv_weight": bell_draw(key_of[4], (SECTIONS, D, 2 * KVW), D ** -0.5, 0.0625, ((0, 16), (1, 32))),
        "stream": draw_stream(jax.random.fold_in(key_of[8], 71), 0),
        "norm_gain": jnp.clip(1.0 + 0.18 * jax.random.normal(key_of[6], (D,), jnp.float32), 0.1, 1.9),
        "lengths": draw_lengths(jax.random.fold_in(key_of[8], 71), 0),
    }


NORM_EPS = 1e-05

def section_grads(query_rows, grad_rows, key_rows, value_rows):
    group_size = HQ // KVH
    score_scale = 1.0 / math.sqrt(HD)
    query_h = query_rows.reshape(GROUPS, TXT, KVH, group_size, HD).astype(jnp.float32)
    grad_h = grad_rows.reshape(GROUPS, TXT, KVH, group_size, HD).astype(jnp.float32)
    key_h = key_rows.reshape(GROUPS, LAT, KVH, HD).astype(jnp.float32)
    value_h = value_rows.reshape(GROUPS, LAT, KVH, HD).astype(jnp.float32)
    scores = jnp.einsum('mtgqd,mjgd->mgqjt', query_h, key_h) * score_scale
    row_max = lax.optimization_barrier(jnp.max(scores, axis=3, keepdims=True))
    expo = jnp.exp(scores - row_max)
    prob_values = expo / lax.optimization_barrier(jnp.sum(expo, axis=3, keepdims=True))
    dprob = jnp.einsum('mtgqd,mjgd->mgqjt', grad_h, value_h)
    centre = lax.optimization_barrier(jnp.sum(prob_values * dprob, axis=3, keepdims=True))
    dscore = lax.optimization_barrier((prob_values * (dprob - centre) * score_scale).astype(jnp.bfloat16)).astype(jnp.float32)
    probs_b = lax.optimization_barrier(prob_values.astype(jnp.bfloat16)).astype(jnp.float32)
    key_grad = jnp.einsum('mgqjt,mtgqd->mjgd', dscore, query_h)
    value_grad = jnp.einsum('mgqjt,mtgqd->mjgd', probs_b, grad_h)
    joined = jnp.concatenate([key_grad.reshape(GROUPS * LAT, KVH * HD), value_grad.reshape(GROUPS * LAT, KVH * HD)], axis=1)
    return joined.astype(jnp.bfloat16)

def reference(queries, out_grad, keys, values, kv_weight, stream, norm_gain, lengths):
    token_ids = jnp.arange(GROUPS * TXT, dtype=jnp.int32)
    token_live = token_ids % TXT < lengths[token_ids // TXT]
    masked_grad = jnp.where(token_live[None, :, None], out_grad, jnp.zeros_like(out_grad))
    promoted = stream.astype(jnp.float32)
    inverse = lax.rsqrt(lax.optimization_barrier(jnp.mean(promoted * promoted, axis=1, keepdims=True)) + NORM_EPS)
    normed = promoted * inverse
    latents = (normed * norm_gain[None, :]).astype(jnp.bfloat16)

    def one_section(summed, items):
        query_rows, grad_rows, key_rows, value_rows, weight = items
        kv_grads = section_grads(query_rows, grad_rows, key_rows, value_rows)
        weight_grad = jnp.dot(latents.T, kv_grads, preferred_element_type=jnp.float32) / GROUPS
        term = lax.dot_general(kv_grads, weight, (((1,), (1,)), ((), ())), preferred_element_type=jnp.float32)
        return (summed + term, weight_grad)
    start_sum = jnp.zeros((GROUPS * LAT, D), jnp.float32)
    section_sum, weight_grads = lax.scan(one_section, start_sum, (queries, masked_grad, keys, values, kv_weight))
    latent_grad = section_sum.astype(jnp.bfloat16)
    gain_grad = lax.optimization_barrier(jnp.sum(section_sum * normed, axis=0)) / GROUPS
    return (weight_grads, latent_grad, gain_grad)
```

```python
import math

import jax
import jax.numpy as jnp
from jax import lax
from jax.experimental import pallas as pl
from jax.experimental.pallas import tpu as pltpu
from jax.sharding import PartitionSpec as P

D = 8192
HQ = 32
KVH = 4
HD = 128


NORM_EPS = 1e-05


def attention_grads(query_rows, grad_rows, key_rows, value_rows, length):
    token_count = query_rows.shape[0]
    latent_count = key_rows.shape[0]
    group_size = HQ // KVH
    score_scale = 1.0 / math.sqrt(HD)
    token_live = lax.iota(jnp.int32, token_count) < length
    masked = jnp.where(token_live[:, None], grad_rows, jnp.zeros_like(grad_rows))
    query_h = query_rows.reshape(token_count, KVH, group_size, HD)
    grad_h = masked.reshape(token_count, KVH, group_size, HD)
    key_h = key_rows.reshape(latent_count, KVH, HD)
    value_h = value_rows.reshape(latent_count, KVH, HD)
    scores = (
        jnp.einsum("tgqd,jgd->gqjt", query_h, key_h, preferred_element_type=jnp.float32)
        * score_scale
    )
    row_max = jnp.max(scores, axis=2, keepdims=True)
    expo = jnp.exp(scores - row_max)
    prob_values = expo / jnp.sum(expo, axis=2, keepdims=True)
    dprob = jnp.einsum("tgqd,jgd->gqjt", grad_h, value_h, preferred_element_type=jnp.float32)
    centre = jnp.sum(prob_values * dprob, axis=2, keepdims=True)
    dscore = (prob_values * (dprob - centre) * score_scale).astype(jnp.bfloat16)
    probs_b = prob_values.astype(jnp.bfloat16)
    key_grad = jnp.einsum("gqjt,tgqd->jgd", dscore, query_h, preferred_element_type=jnp.float32)
    value_grad = jnp.einsum("gqjt,tgqd->jgd", probs_b, grad_h, preferred_element_type=jnp.float32)
    joined = jnp.concatenate(
        [key_grad.reshape(latent_count, KVH * HD), value_grad.reshape(latent_count, KVH * HD)],
        axis=1,
    )
    return joined.astype(jnp.bfloat16)


ROWS = 2048
COLS = 256
KVC = 1024
LAT = 64
HALF = 32
PIPE = 16
GROUPS = 32
SHARE = 128

GATHER = ["Zp0", "Zm1", "Zp1", "Zm0", "Fp0", "Fm1"]
GATHER += [n + str(i) for i in range(4) for n in ("Xp0", "Xm1", "Xp1", "Xm0", "Gp0", "Gm1")]
GATHER += ["C%d%d" % (i, j) for i in range(4) for j in range(4)]
OTHERS = ["Qz1", "Qz2", "Qz3", "Qx1", "Qx2", "Qx3", "Qc"]
OTHERS += [n + str(i) for i in range(4) for n in ("Yo", "Yn", "Yr")]
OTHERS += ["L1", "L2", "L3", "Gy1", "Gy2", "Gy3", "Gl1", "Gl2", "Gl3"]
SLOT = {n: i for i, n in enumerate(GATHER + OTHERS)}


def exchange_kernel(
    kv_ref, w_ref, st_ref, gn_ref, wg_ref, lat_ref, gain_ref,
    g, xt, latt, sq, sqz, sqx, sqc, sqs, inv, tf, tb, ro, rp, rm, sr, sl, rl, gs, gy, gs2, gl,
    send_sem, recv_sem,
):
    p = lax.axis_index("pipe")
    q = lax.axis_index("dp")
    zl, y = lax.div(p, 4), lax.rem(p, 4)
    zh, x, c = lax.div(q, 8), lax.rem(lax.div(q, 2), 4), lax.rem(q, 2)

    def up(a, k):
        return lax.rem(a + k + 4, 4)

    def dp_dev(zz, xx, cc):
        return (p, zz * 8 + xx * 2 + cc)

    def pipe_dev(zz, yy):
        return (zz * 4 + yy, q)

    z_dev = {k: dp_dev(up(zh, k), x, c) for k in (1, 2, 3)}
    x_dev = {k: dp_dev(zh, up(x, k), c) for k in (1, 2, 3)}
    c_dev = dp_dev(zh, x, 1 - c)
    y_dev = {k: pipe_dev(zl, up(y, k)) for k in (1, 2, 3)}
    l_dev = {k: pipe_dev(up(zl, k), y) for k in (1, 2, 3)}
    peers = [*z_dev.values(), *x_dev.values(), c_dev, *y_dev.values(), *l_dev.values()]

    barrier = pltpu.get_barrier_semaphore()
    for peer in peers:
        pl.semaphore_signal(barrier, inc=1, device_id=peer, device_id_type=pl.DeviceIdType.MESH)

    started = []

    def copy(name, src, dst, dev):
        s = SLOT[name]
        return pltpu.make_async_remote_copy(
            src_ref=src, dst_ref=dst, send_sem=send_sem.at[s], recv_sem=recv_sem.at[s],
            device_id=dev, device_id_type=pl.DeviceIdType.MESH,
        )

    def send(name, src, dst, dev):
        made = copy(name, src, dst, dev)
        made.start()
        started.append(made)

    def arrive(name, dst):
        copy(name, dst, dst, c_dev).wait_recv()

    def rows_of(zz, xx, cc, half):
        start = ((zz * 4 + xx) * 2 + cc) * LAT
        if half is None:
            return pl.ds(pl.multiple_of(start, LAT), LAT)
        return pl.ds(pl.multiple_of(start + half * HALF, HALF), HALF)

    zs = [zh, up(zh, -1), up(zh, 1), up(zh, 2)]
    xs = [x, up(x, -1), up(x, 1), up(x, 2)]

    def block(zi, xi, half):
        return g.at[rows_of(zs[zi], xs[xi], c, half)]

    def own(half):
        return kv_ref.at[pl.ds(half * HALF, HALF)]

    def squares(i, carry):
        rows = pl.ds(pl.multiple_of(i * 128, 128), 128)
        turned = st_ref[rows, :].astype(jnp.float32).T
        xt[:, rows] = turned.astype(jnp.bfloat16)
        sq[pl.ds(i, 1), :] = jnp.sum(turned * turned, axis=0, keepdims=True)
        return carry

    lax.fori_loop(0, ROWS // 128, squares, 0)
    pl.semaphore_wait(barrier, len(peers))

    for name, half, dev in (("Zp0", 0, 1), ("Zm1", 1, 3), ("Zp1", 1, 1), ("Zm0", 0, 3)):
        send(name, own(half), block(0, 0, half), z_dev[dev])
    for k in (1, 2, 3):
        send("Qz%d" % k, sq, sqz.at[k - 1], z_dev[k])
    for name, half, dev in (("Xp00", 0, 1), ("Xm10", 1, 3), ("Xp10", 1, 1), ("Xm00", 0, 3)):
        send(name, own(half), block(0, 0, half), x_dev[dev])
    send("C00", kv_ref, block(0, 0, None), c_dev)
    g[rows_of(zh, x, c, None), :] = kv_ref[...]

    def x_send(zi, half):
        b = block(zi, 0, half)
        send("Xp%d%d" % (half, zi), b, b, x_dev[1])
        send("Xm%d%d" % (half, zi), b, b, x_dev[3])

    def core_send(zi, xi):
        b = block(zi, xi, None)
        send("C%d%d" % (zi, xi), b, b, c_dev)

    def x_near(zi):
        arrive("Xp0%d" % zi, block(zi, 1, 0))
        send("Gp0%d" % zi, block(zi, 1, 0), block(zi, 1, 0), x_dev[1])
        arrive("Xm1%d" % zi, block(zi, 2, 1))
        send("Gm1%d" % zi, block(zi, 2, 1), block(zi, 2, 1), x_dev[3])
        arrive("Xp1%d" % zi, block(zi, 1, 1))
        core_send(zi, 1)
        arrive("Xm0%d" % zi, block(zi, 2, 0))
        core_send(zi, 2)

    def x_far(zi):
        arrive("Gp0%d" % zi, block(zi, 3, 0))
        arrive("Gm1%d" % zi, block(zi, 3, 1))
        core_send(zi, 3)

    x_near(0)
    x_far(0)
    arrive("Zp0", block(1, 0, 0))
    send("Fp0", block(1, 0, 0), block(1, 0, 0), z_dev[1])
    x_send(1, 0)
    arrive("Zm1", block(2, 0, 1))
    send("Fm1", block(2, 0, 1), block(2, 0, 1), z_dev[3])
    x_send(2, 1)
    arrive("Zp1", block(1, 0, 1))
    x_send(1, 1)
    core_send(1, 0)
    arrive("Zm0", block(2, 0, 0))
    x_send(2, 0)
    core_send(2, 0)
    for k in (1, 2, 3):
        arrive("Qz%d" % k, sqz.at[k - 1])
    sqs[0] = sq[...] + sqz[0] + sqz[1] + sqz[2]
    for k in (1, 2, 3):
        send("Qx%d" % k, sqs.at[0], sqx.at[k - 1], x_dev[k])
    x_near(1)
    x_near(2)
    for k in (1, 2, 3):
        arrive("Qx%d" % k, sqx.at[k - 1])
    sqs[1] = sqs[0] + sqx[0] + sqx[1] + sqx[2]
    send("Qc", sqs.at[1], sqc, c_dev)
    arrive("Fp0", block(3, 0, 0))
    x_send(3, 0)
    arrive("Fm1", block(3, 0, 1))
    x_send(3, 1)
    core_send(3, 0)
    x_far(1)
    x_far(2)
    arrive("Qc", sqc)
    inv[...] = lax.rsqrt((sqs[1] + sqc[...]) / D + NORM_EPS)

    def normalise(i, carry):
        rows = pl.ds(pl.multiple_of(i * 128, 128), 128)
        normed = xt[:, rows].astype(jnp.float32) * inv[pl.ds(i, 1), :]
        latt[:, rows] = (normed * gn_ref[...]).astype(jnp.bfloat16)
        return carry

    lax.fori_loop(0, ROWS // 128, normalise, 0)
    x_near(3)
    x_far(3)
    for zi in range(4):
        for xi in range(4):
            arrive("C%d%d" % (zi, xi), g.at[rows_of(zs[zi], xs[xi], 1 - c, None)])

    def piece(level, yy):
        return pl.ds(pl.multiple_of((level * 4 + yy) * SHARE, SHARE), SHARE)

    def level_rows(level):
        return pl.ds(level * SHARE, SHARE)

    yo, yp, ym = up(y, 2), up(y, 1), up(y, -1)
    for level in (0, 2, 1, 3):
        rows = pl.ds(level * 512, 512)
        terms = lax.dot_general(
            g[rows, :], w_ref[...], (((1,), (1,)), ((), ())), preferred_element_type=jnp.float32
        )
        tf[rows, :] = terms
        tb[rows, :] = terms.astype(jnp.bfloat16)
        low = level < 2
        there = y_dev[1] if low else y_dev[3]
        back = y_dev[3] if low else y_dev[1]
        send("Yo%d" % level, tb.at[piece(level, yo)], ro.at[level_rows(level)], there)
        into = rm if low else rp
        send("Yn%d" % level, tb.at[piece(level, ym if low else yp)], into.at[level_rows(level)], back)
    for level in (0, 2, 1, 3):
        low = level < 2
        arrive("Yo%d" % level, ro.at[level_rows(level)])
        mine = tf[piece(level, yp if low else ym), :]
        relayed = mine + ro[level_rows(level), :].astype(jnp.float32)
        sr[level_rows(level), :] = relayed.astype(jnp.bfloat16)
        into = rp if low else rm
        send("Yr%d" % level, sr.at[level_rows(level)], into.at[level_rows(level)], y_dev[1] if low else y_dev[3])

    def weight_tile(i, carry):
        cols = pl.ds(pl.multiple_of(i * 256, 256), 256)
        wg_ref[:, cols] = jnp.dot(latt[...], g[:, cols], preferred_element_type=jnp.float32) / GROUPS
        return carry

    lax.fori_loop(0, KVC // 256, weight_tile, 0)

    for level in range(4):
        arrive("Yn%d" % level, (rm if level < 2 else rp).at[level_rows(level)])
        arrive("Yr%d" % level, (rp if level < 2 else rm).at[level_rows(level)])

    def reduced(level):
        part = pl.ds(pl.multiple_of(level * SHARE, SHARE), SHARE)
        return tf[piece(level, y), :] + rp[part, :].astype(jnp.float32) + rm[part, :].astype(jnp.float32)

    for k in (3, 2, 1):
        sl[k - 1] = reduced(up(zl, k)).astype(jnp.bfloat16)
        send("L%d" % k, sl.at[k - 1], rl.at[k - 1], l_dev[k])
    share = reduced(zl)
    own_inverse = jnp.broadcast_to(inv[pl.ds(p, 1), :], (128, 128)).T
    own_stream = st_ref[pl.ds(pl.multiple_of(p * SHARE, SHARE), SHARE), :].astype(jnp.float32)
    normed = own_stream * jnp.concatenate([own_inverse, own_inverse], axis=1)
    for k in (1, 2, 3):
        arrive("L%d" % k, rl.at[k - 1])
        share = share + rl[k - 1].astype(jnp.float32)
    lat_ref[...] = share.astype(jnp.bfloat16)
    part = jnp.sum(share * normed, axis=0, keepdims=True)
    gs[...] = jnp.broadcast_to(part, (8, COLS))
    for k in (1, 2, 3):
        send("Gy%d" % k, gs, gy.at[k - 1], y_dev[k])
    for k in (1, 2, 3):
        arrive("Gy%d" % k, gy.at[k - 1])
    gs2[...] = gs[...] + gy[0] + gy[1] + gy[2]
    for k in (1, 2, 3):
        send("Gl%d" % k, gs2, gl.at[k - 1], l_dev[k])
    for k in (1, 2, 3):
        arrive("Gl%d" % k, gl.at[k - 1])
    gain_ref[...] = (gs2[...] + gl[0] + gl[1] + gl[2]) / GROUPS
    for made in started:
        made.wait_send()


def exchange(kv_grads, weight, stream, gain):
    f32, bf16 = jnp.float32, jnp.bfloat16
    vmem = pl.BlockSpec(memory_space=pltpu.VMEM)
    count = len(SLOT)
    return pl.pallas_call(
        exchange_kernel,
        out_shape=(
            jax.ShapeDtypeStruct((COLS, KVC), f32),
            jax.ShapeDtypeStruct((SHARE, COLS), bf16),
            jax.ShapeDtypeStruct((8, COLS), f32),
        ),
        in_specs=[vmem] * 4,
        out_specs=(vmem,) * 3,
        scratch_shapes=[
            pltpu.VMEM((ROWS, KVC), bf16),
            pltpu.VMEM((COLS, ROWS), bf16),
            pltpu.VMEM((COLS, ROWS), bf16),
            pltpu.VMEM((16, 128), f32),
            pltpu.VMEM((3, 16, 128), f32),
            pltpu.VMEM((3, 16, 128), f32),
            pltpu.VMEM((16, 128), f32),
            pltpu.VMEM((2, 16, 128), f32),
            pltpu.VMEM((16, 128), f32),
            pltpu.VMEM((ROWS, COLS), f32),
            pltpu.VMEM((ROWS, COLS), bf16),
            pltpu.VMEM((512, COLS), bf16),
            pltpu.VMEM((512, COLS), bf16),
            pltpu.VMEM((512, COLS), bf16),
            pltpu.VMEM((512, COLS), bf16),
            pltpu.VMEM((3, SHARE, COLS), bf16),
            pltpu.VMEM((3, SHARE, COLS), bf16),
            pltpu.VMEM((8, COLS), f32),
            pltpu.VMEM((3, 8, COLS), f32),
            pltpu.VMEM((8, COLS), f32),
            pltpu.VMEM((3, 8, COLS), f32),
            pltpu.SemaphoreType.DMA((count,)),
            pltpu.SemaphoreType.DMA((count,)),
        ],
        compiler_params=pltpu.CompilerParams(
            collective_id=0, has_side_effects=True, vmem_limit_bytes=48 * 1024 * 1024
        ),
        name="exchange",
    )(kv_grads, weight, stream, gain)


def body(queries, out_grad, keys, values, kv_weight, stream, norm_gain, lengths):
    kv_grads = attention_grads(queries[0], out_grad[0], keys[0], values[0], lengths[0])
    gain = jnp.broadcast_to(norm_gain[:, None], (COLS, 128))
    weight_grad, latent_grad, gain_grad = exchange(kv_grads, kv_weight[0], stream, gain)
    return (weight_grad[None], latent_grad, gain_grad[0])


def solution(mesh):
    return jax.shard_map(
        body,
        mesh=mesh,
        in_specs=(
            P("pipe", "dp", None),
            P("pipe", "dp", None),
            P("pipe", "dp", None),
            P("pipe", "dp", None),
            P("pipe", "dp", None),
            P(None, "dp"),
            P("dp"),
            P("dp"),
        ),
        out_specs=(P("pipe", "dp", None), P("pipe", "dp"), P("dp")),
        check_vma=False,
    )
```

```python
import math

import jax
import jax.numpy as jnp
from jax import lax
from jax.experimental import pallas as pl
from jax.experimental.pallas import tpu as pltpu
from jax.sharding import PartitionSpec as P

D = 8192
HQ = 32
KVH = 4
HD = 128


NORM_EPS = 1e-05


def attention_grads(query_rows, grad_rows, key_rows, value_rows, length):
    token_count = query_rows.shape[0]
    latent_count = key_rows.shape[0]
    group_size = HQ // KVH
    score_scale = 1.0 / math.sqrt(HD)
    token_live = lax.iota(jnp.int32, token_count) < length
    masked = jnp.where(token_live[:, None], grad_rows, jnp.zeros_like(grad_rows))
    query_h = query_rows.reshape(token_count, KVH, group_size, HD)
    grad_h = masked.reshape(token_count, KVH, group_size, HD)
    key_h = key_rows.reshape(latent_count, KVH, HD)
    value_h = value_rows.reshape(latent_count, KVH, HD)
    scores = (
        jnp.einsum("tgqd,jgd->gqjt", query_h, key_h, preferred_element_type=jnp.float32)
        * score_scale
    )
    row_max = jnp.max(scores, axis=2, keepdims=True)
    expo = jnp.exp(scores - row_max)
    prob_values = expo / jnp.sum(expo, axis=2, keepdims=True)
    dprob = jnp.einsum("tgqd,jgd->gqjt", grad_h, value_h, preferred_element_type=jnp.float32)
    centre = jnp.sum(prob_values * dprob, axis=2, keepdims=True)
    dscore = (prob_values * (dprob - centre) * score_scale).astype(jnp.bfloat16)
    probs_b = prob_values.astype(jnp.bfloat16)
    key_grad = jnp.einsum("gqjt,tgqd->jgd", dscore, query_h, preferred_element_type=jnp.float32)
    value_grad = jnp.einsum("gqjt,tgqd->jgd", probs_b, grad_h, preferred_element_type=jnp.float32)
    joined = jnp.concatenate(
        [key_grad.reshape(latent_count, KVH * HD), value_grad.reshape(latent_count, KVH * HD)],
        axis=1,
    )
    return joined.astype(jnp.bfloat16)


ROWS = 2048
COLS = 256
KVC = 1024
LAT = 64
HALF = 32
PIPE = 16
GROUPS = 32
SHARE = 128

GATHER = ["Zp0", "Zm1", "Zp1", "Zm0", "Fp0", "Fm1"]
GATHER += [n + str(i) for i in range(4) for n in ("Xp0", "Xm1", "Xp1", "Xm0", "Gp0", "Gm1")]
GATHER += ["C%d%d" % (i, j) for i in range(4) for j in range(4)]
OTHERS = ["Qz1", "Qz2", "Qz3", "Qx1", "Qx2", "Qx3", "Qc"]
OTHERS += [n + str(h) + str(i) for i in range(4) for h in range(2) for n in ("Yo", "Yn", "Yr")]
OTHERS += ["L1", "L2", "L3", "Gy1", "Gy2", "Gy3", "Gl1", "Gl2", "Gl3"]
SLOT = {n: i for i, n in enumerate(GATHER + OTHERS)}


def exchange_kernel(
    kv_ref, w_ref, st_ref, gn_ref, wg_ref, lat_ref, gain_ref,
    g, xt, latt, sq, sqz, sqx, sqc, sqs, inv, tf, tb, ro, rp, rm, sr, sl, rl, gs, gy, gs2, gl, share_ref,
    send_sem, recv_sem,
):
    p = lax.axis_index("pipe")
    q = lax.axis_index("dp")
    zl, y = lax.div(p, 4), lax.rem(p, 4)
    zh, x, c = lax.div(q, 8), lax.rem(lax.div(q, 2), 4), lax.rem(q, 2)

    def up(a, k):
        return lax.rem(a + k + 4, 4)

    def dp_dev(zz, xx, cc):
        return (p, zz * 8 + xx * 2 + cc)

    def pipe_dev(zz, yy):
        return (zz * 4 + yy, q)

    z_dev = {k: dp_dev(up(zh, k), x, c) for k in (1, 2, 3)}
    x_dev = {k: dp_dev(zh, up(x, k), c) for k in (1, 2, 3)}
    c_dev = dp_dev(zh, x, 1 - c)
    y_dev = {k: pipe_dev(zl, up(y, k)) for k in (1, 2, 3)}
    l_dev = {k: pipe_dev(up(zl, k), y) for k in (1, 2, 3)}
    peers = [*z_dev.values(), *x_dev.values(), c_dev, *y_dev.values(), *l_dev.values()]

    barrier = pltpu.get_barrier_semaphore()
    for peer in peers:
        pl.semaphore_signal(barrier, inc=1, device_id=peer, device_id_type=pl.DeviceIdType.MESH)

    started = []

    def copy(name, src, dst, dev):
        s = SLOT[name]
        return pltpu.make_async_remote_copy(
            src_ref=src, dst_ref=dst, send_sem=send_sem.at[s], recv_sem=recv_sem.at[s],
            device_id=dev, device_id_type=pl.DeviceIdType.MESH,
        )

    def send(name, src, dst, dev):
        made = copy(name, src, dst, dev)
        made.start()
        started.append(made)

    def arrive(name, dst):
        copy(name, dst, dst, c_dev).wait_recv()

    def rows_of(zz, xx, cc, half):
        start = ((zz * 4 + xx) * 2 + cc) * LAT
        if half is None:
            return pl.ds(pl.multiple_of(start, LAT), LAT)
        return pl.ds(pl.multiple_of(start + half * HALF, HALF), HALF)

    zs = [zh, up(zh, -1), up(zh, 1), up(zh, 2)]
    xs = [x, up(x, -1), up(x, 1), up(x, 2)]

    def block(zi, xi, half):
        return g.at[rows_of(zs[zi], xs[xi], c, half)]

    def own(half):
        return kv_ref.at[pl.ds(half * HALF, HALF)]

    def squares(i, carry):
        rows = pl.ds(pl.multiple_of(i * 128, 128), 128)
        turned = st_ref[rows, :].astype(jnp.float32).T
        xt[:, rows] = turned.astype(jnp.bfloat16)
        sq[pl.ds(i, 1), :] = jnp.sum(turned * turned, axis=0, keepdims=True)
        return carry

    pl.semaphore_wait(barrier, len(peers))

    for name, half, dev in (("Zp0", 0, 1), ("Zm1", 1, 3), ("Zp1", 1, 1), ("Zm0", 0, 3)):
        send(name, own(half), block(0, 0, half), z_dev[dev])
    for name, half, dev in (("Xp00", 0, 1), ("Xm10", 1, 3), ("Xp10", 1, 1), ("Xm00", 0, 3)):
        send(name, own(half), block(0, 0, half), x_dev[dev])
    send("C00", kv_ref, block(0, 0, None), c_dev)
    g[rows_of(zh, x, c, None), :] = kv_ref[...]
    lax.fori_loop(0, ROWS // 128, squares, 0)
    for k in (1, 2, 3):
        send("Qz%d" % k, sq, sqz.at[k - 1], z_dev[k])

    def x_send(zi, half):
        b = block(zi, 0, half)
        send("Xp%d%d" % (half, zi), b, b, x_dev[1])
        send("Xm%d%d" % (half, zi), b, b, x_dev[3])

    def core_send(zi, xi):
        b = block(zi, xi, None)
        send("C%d%d" % (zi, xi), b, b, c_dev)

    def x_near(zi):
        arrive("Xp0%d" % zi, block(zi, 1, 0))
        send("Gp0%d" % zi, block(zi, 1, 0), block(zi, 1, 0), x_dev[1])
        arrive("Xm1%d" % zi, block(zi, 2, 1))
        send("Gm1%d" % zi, block(zi, 2, 1), block(zi, 2, 1), x_dev[3])
        arrive("Xp1%d" % zi, block(zi, 1, 1))
        core_send(zi, 1)
        arrive("Xm0%d" % zi, block(zi, 2, 0))
        core_send(zi, 2)

    def x_far(zi):
        arrive("Gp0%d" % zi, block(zi, 3, 0))
        arrive("Gm1%d" % zi, block(zi, 3, 1))
        core_send(zi, 3)

    yo, yp, ym = up(y, 2), up(y, 1), up(y, -1)

    def level_rows(zi, base=0, size=512):
        return pl.ds(pl.multiple_of(zs[zi] * 512 + base, size), size)

    def part(zi, yy, half):
        return pl.ds(pl.multiple_of(zi * 512 + yy * SHARE + half * LAT, LAT), LAT)

    def slot(zi, half):
        return pl.ds(zi * SHARE + half * LAT, LAT)

    def terms(zi):
        for xi in range(4):
            arrive("C%d%d" % (zi, xi), g.at[rows_of(zs[zi], xs[xi], 1 - c, None)])
        made = lax.dot_general(
            g[level_rows(zi), :], w_ref[...], (((1,), (1,)), ((), ())), preferred_element_type=jnp.float32
        )
        rows = pl.ds(zi * 512, 512)
        tf[rows, :] = made
        tb[rows, :] = made.astype(jnp.bfloat16)
        send("Yo0%d" % zi, tb.at[part(zi, yo, 0)], ro.at[slot(zi, 0)], y_dev[1])
        send("Yo1%d" % zi, tb.at[part(zi, yo, 1)], ro.at[slot(zi, 1)], y_dev[3])
        send("Yn0%d" % zi, tb.at[part(zi, ym, 0)], rm.at[slot(zi, 0)], y_dev[3])
        send("Yn1%d" % zi, tb.at[part(zi, yp, 1)], rp.at[slot(zi, 1)], y_dev[1])

    def relay(zi):
        for half, to, into, dev in ((0, yp, rp, 1), (1, ym, rm, 3)):
            arrive("Yo%d%d" % (half, zi), ro.at[slot(zi, half)])
            total = tf[part(zi, to, half), :] + ro[slot(zi, half), :].astype(jnp.float32)
            sr[slot(zi, half), :] = total.astype(jnp.bfloat16)
            send("Yr%d%d" % (half, zi), sr.at[slot(zi, half)], into.at[slot(zi, half)], y_dev[dev])

    level_sends = []

    def settle(zi):
        for half, near, far in ((0, rm, rp), (1, rp, rm)):
            arrive("Yn%d%d" % (half, zi), near.at[slot(zi, half)])
            arrive("Yr%d%d" % (half, zi), far.at[slot(zi, half)])
        mine = pl.ds(pl.multiple_of(zi * 512 + y * SHARE, SHARE), SHARE)
        got = pl.ds(zi * SHARE, SHARE)
        total = tf[mine, :] + rp[got, :].astype(jnp.float32) + rm[got, :].astype(jnp.float32)
        k = up(zs[zi] - zl, 0)

        @pl.when(k == 0)
        def _():
            share_ref[...] = total

        made = pltpu.make_async_remote_copy(
            src_ref=sl.at[zi], dst_ref=rl.at[lax.max(k, 1) - 1],
            send_sem=send_sem.at[SLOT["L1"] + lax.max(k, 1) - 1],
            recv_sem=recv_sem.at[SLOT["L1"] + lax.max(k, 1) - 1],
            device_id=pipe_dev(zs[zi], y), device_id_type=pl.DeviceIdType.MESH,
        )

        @pl.when(k != 0)
        def _():
            sl[zi] = total.astype(jnp.bfloat16)
            made.start()

        level_sends.append((k, made))

    def weight_part(zi):
        def tile(i, carry):
            cols = pl.ds(pl.multiple_of(i * 256, 256), 256)
            made = jnp.dot(
                latt[:, level_rows(zi)], g[level_rows(zi), cols], preferred_element_type=jnp.float32
            )
            if zi == 0:
                wg_ref[:, cols] = made
            elif zi < 3:
                wg_ref[:, cols] = wg_ref[:, cols] + made
            else:
                wg_ref[:, cols] = (wg_ref[:, cols] + made) / GROUPS
            return carry

        lax.fori_loop(0, KVC // 256, tile, 0)

    def gain_part(zi, total):
        for j in range(4):
            rows = pl.ds(pl.multiple_of(zs[zi] * 512 + j * 128, 128), 128)
            scale = jnp.broadcast_to(inv[pl.ds(zs[zi] * 4 + j, 1), :], (128, 128)).T
            normed = st_ref[rows, :].astype(jnp.float32) * jnp.concatenate([scale, scale], axis=1)
            total = total + jnp.sum(tf[pl.ds(zi * 512 + j * 128, 128), :] * normed, axis=0, keepdims=True)
        return total

    def normalise(i, carry):
        rows = pl.ds(pl.multiple_of(i * 128, 128), 128)
        normed = xt[:, rows].astype(jnp.float32) * inv[pl.ds(i, 1), :]
        latt[:, rows] = (normed * gn_ref[...]).astype(jnp.bfloat16)
        return carry

    x_near(0)
    x_far(0)
    terms(0)
    relay(0)
    arrive("Zp0", block(1, 0, 0))
    send("Fp0", block(1, 0, 0), block(1, 0, 0), z_dev[1])
    x_send(1, 0)
    arrive("Zm1", block(2, 0, 1))
    send("Fm1", block(2, 0, 1), block(2, 0, 1), z_dev[3])
    x_send(2, 1)
    arrive("Zp1", block(1, 0, 1))
    x_send(1, 1)
    core_send(1, 0)
    arrive("Zm0", block(2, 0, 0))
    x_send(2, 0)
    core_send(2, 0)
    for k in (1, 2, 3):
        arrive("Qz%d" % k, sqz.at[k - 1])
    sqs[0] = sq[...] + sqz[0] + sqz[1] + sqz[2]
    for k in (1, 2, 3):
        send("Qx%d" % k, sqs.at[0], sqx.at[k - 1], x_dev[k])
    settle(0)
    x_near(1)
    x_near(2)
    for k in (1, 2, 3):
        arrive("Qx%d" % k, sqx.at[k - 1])
    sqs[1] = sqs[0] + sqx[0] + sqx[1] + sqx[2]
    send("Qc", sqs.at[1], sqc, c_dev)
    arrive("Fp0", block(3, 0, 0))
    x_send(3, 0)
    arrive("Fm1", block(3, 0, 1))
    x_send(3, 1)
    core_send(3, 0)
    x_far(1)
    x_far(2)
    terms(1)
    terms(2)
    arrive("Qc", sqc)
    inv[...] = lax.rsqrt((sqs[1] + sqc[...]) / D + NORM_EPS)
    x_near(3)
    relay(1)
    relay(2)
    lax.fori_loop(0, ROWS // 128, normalise, 0)
    x_far(3)
    settle(1)
    settle(2)
    terms(3)
    part_sum = jnp.zeros((1, COLS), jnp.float32)
    for zi in range(4):
        part_sum = gain_part(zi, part_sum)
    gs[...] = jnp.broadcast_to(part_sum, (8, COLS))
    for k in (1, 2, 3):
        send("Gy%d" % k, gs, gy.at[k - 1], y_dev[k])
    relay(3)
    weight_part(0)
    weight_part(1)
    settle(3)
    for k in (1, 2, 3):
        arrive("Gy%d" % k, gy.at[k - 1])
    gs2[...] = gs[...] + gy[0] + gy[1] + gy[2]
    for k in (1, 2, 3):
        send("Gl%d" % k, gs2, gl.at[k - 1], l_dev[k])
    weight_part(2)
    weight_part(3)
    share = share_ref[...]
    for k in (1, 2, 3):
        arrive("L%d" % k, rl.at[k - 1])
        share = share + rl[k - 1].astype(jnp.float32)
    lat_ref[...] = share.astype(jnp.bfloat16)
    for k in (1, 2, 3):
        arrive("Gl%d" % k, gl.at[k - 1])
    gain_ref[...] = ((gs2[...] + gl[0] + gl[1] + gl[2]) / GROUPS)[0:1]
    for k, made in level_sends:
        @pl.when(k != 0)
        def _(made=made):
            made.wait_send()
    for made in started:
        made.wait_send()


def exchange(kv_grads, weight, stream, gain):
    f32, bf16 = jnp.float32, jnp.bfloat16
    vmem = pl.BlockSpec(memory_space=pltpu.VMEM)
    count = len(SLOT)
    return pl.pallas_call(
        exchange_kernel,
        out_shape=(
            jax.ShapeDtypeStruct((COLS, KVC), f32),
            jax.ShapeDtypeStruct((SHARE, COLS), bf16),
            jax.ShapeDtypeStruct((1, COLS), f32),
        ),
        in_specs=[vmem] * 4,
        out_specs=(vmem,) * 3,
        scratch_shapes=[
            pltpu.VMEM((ROWS, KVC), bf16),
            pltpu.VMEM((COLS, ROWS), bf16),
            pltpu.VMEM((COLS, ROWS), bf16),
            pltpu.VMEM((16, 128), f32),
            pltpu.VMEM((3, 16, 128), f32),
            pltpu.VMEM((3, 16, 128), f32),
            pltpu.VMEM((16, 128), f32),
            pltpu.VMEM((2, 16, 128), f32),
            pltpu.VMEM((16, 128), f32),
            pltpu.VMEM((ROWS, COLS), f32),
            pltpu.VMEM((ROWS, COLS), bf16),
            pltpu.VMEM((512, COLS), bf16),
            pltpu.VMEM((512, COLS), bf16),
            pltpu.VMEM((512, COLS), bf16),
            pltpu.VMEM((512, COLS), bf16),
            pltpu.VMEM((4, SHARE, COLS), bf16),
            pltpu.VMEM((3, SHARE, COLS), bf16),
            pltpu.VMEM((8, COLS), f32),
            pltpu.VMEM((3, 8, COLS), f32),
            pltpu.VMEM((8, COLS), f32),
            pltpu.VMEM((3, 8, COLS), f32),
            pltpu.VMEM((SHARE, COLS), f32),
            pltpu.SemaphoreType.DMA((count,)),
            pltpu.SemaphoreType.DMA((count,)),
        ],
        compiler_params=pltpu.CompilerParams(
            collective_id=0, has_side_effects=True, vmem_limit_bytes=48 * 1024 * 1024
        ),
        name="exchange",
    )(kv_grads, weight, stream, gain)


def body(queries, out_grad, keys, values, kv_weight, stream, norm_gain, lengths):
    kv_grads = attention_grads(queries[0], out_grad[0], keys[0], values[0], lengths[0])
    gain = jnp.broadcast_to(norm_gain[:, None], (COLS, 128))
    weight_grad, latent_grad, gain_grad = exchange(kv_grads, kv_weight[0], stream, gain)
    return (weight_grad[None], latent_grad, gain_grad.reshape(COLS))


def solution(mesh):
    return jax.shard_map(
        body,
        mesh=mesh,
        in_specs=(
            P("pipe", "dp", None),
            P("pipe", "dp", None),
            P("pipe", "dp", None),
            P("pipe", "dp", None),
            P("pipe", "dp", None),
            P(None, "dp"),
            P("dp"),
            P("dp"),
        ),
        out_specs=(P("pipe", "dp", None), P("pipe", "dp"), P("dp")),
        check_vma=False,
    )
```

```python
import math

import jax
import jax.numpy as jnp
from jax import lax
from jax.experimental import pallas as pl
from jax.experimental.pallas import tpu as pltpu
from jax.sharding import PartitionSpec as P

D = 8192
HQ = 32
KVH = 4
HD = 128


NORM_EPS = 1e-05


ROWS = 2048
COLS = 256
KVC = 1024
LAT = 64
HALF = 32
PIPE = 16
GROUPS = 32
SHARE = 128
TXT = 128
GQ = HQ // KVH

GATHER = ["Zp0", "Zm1", "Zp1", "Zm0", "Fp0", "Fm1"]
GATHER += [n + str(i) for i in range(4) for n in ("Xp0", "Xm1", "Xp1", "Xm0", "Gp0", "Gm1")]
GATHER += ["C%d%d" % (i, j) for i in range(4) for j in range(4)]
OTHERS = ["Qz1", "Qz2", "Qz3", "Qx1", "Qx2", "Qx3", "Qc"]
OTHERS += [n + str(h) + str(i) for i in range(4) for h in range(2) for n in ("Yo", "Yn", "Yr")]
OTHERS += ["L1", "L2", "L3", "Gy1", "Gy2", "Gy3", "Gl1", "Gl2", "Gl3"]
SLOT = {n: i for i, n in enumerate(GATHER + OTHERS)}


def exchange_kernel(
    len_ref, q_hbm, og_hbm, k_hbm, v_hbm, w_hbm, st_hbm, gn_ref, wg_ref, lat_ref, gain_ref,
    q_ref, og_ref, k_ref, v_ref, w_ref, st_ref, kv_ref, gn_col, load_sem, g, xt, latt, sq, sqz, sqx, sqc, sqs, inv, tf, tb, ro, rp, rm, sr, sl, rl, gs, gy, gs2, gl, share_ref,
    send_sem, recv_sem,
):
    p = lax.axis_index("pipe")
    q = lax.axis_index("dp")
    zl, y = lax.div(p, 4), lax.rem(p, 4)
    zh, x, c = lax.div(q, 8), lax.rem(lax.div(q, 2), 4), lax.rem(q, 2)

    def up(a, k):
        return lax.rem(a + k + 4, 4)

    def dp_dev(zz, xx, cc):
        return (p, zz * 8 + xx * 2 + cc)

    def pipe_dev(zz, yy):
        return (zz * 4 + yy, q)

    z_dev = {k: dp_dev(up(zh, k), x, c) for k in (1, 2, 3)}
    x_dev = {k: dp_dev(zh, up(x, k), c) for k in (1, 2, 3)}
    c_dev = dp_dev(zh, x, 1 - c)
    y_dev = {k: pipe_dev(zl, up(y, k)) for k in (1, 2, 3)}
    l_dev = {k: pipe_dev(up(zl, k), y) for k in (1, 2, 3)}
    peers = [*z_dev.values(), *x_dev.values(), c_dev, *y_dev.values(), *l_dev.values()]

    barrier = pltpu.get_barrier_semaphore()
    for peer in peers:
        pl.semaphore_signal(barrier, inc=1, device_id=peer, device_id_type=pl.DeviceIdType.MESH)

    loads = []
    pairs = ((q_hbm, q_ref), (k_hbm, k_ref), (og_hbm, og_ref), (v_hbm, v_ref), (st_hbm, st_ref), (w_hbm, w_ref))
    for n, (src, dst) in enumerate(pairs):
        load = pltpu.make_async_copy(src, dst, load_sem.at[n])
        load.start()
        loads.append(load)
    started = []

    def copy(name, src, dst, dev):
        s = SLOT[name]
        return pltpu.make_async_remote_copy(
            src_ref=src, dst_ref=dst, send_sem=send_sem.at[s], recv_sem=recv_sem.at[s],
            device_id=dev, device_id_type=pl.DeviceIdType.MESH,
        )

    def send(name, src, dst, dev):
        made = copy(name, src, dst, dev)
        made.start()
        started.append(made)

    def arrive(name, dst):
        copy(name, dst, dst, c_dev).wait_recv()

    def rows_of(zz, xx, cc, half):
        start = ((zz * 4 + xx) * 2 + cc) * LAT
        if half is None:
            return pl.ds(pl.multiple_of(start, LAT), LAT)
        return pl.ds(pl.multiple_of(start + half * HALF, HALF), HALF)

    zs = [zh, up(zh, -1), up(zh, 1), up(zh, 2)]
    xs = [x, up(x, -1), up(x, 1), up(x, 2)]

    def block(zi, xi, half):
        return g.at[rows_of(zs[zi], xs[xi], c, half)]

    def own(half):
        return kv_ref.at[pl.ds(half * HALF, HALF)]

    def squares(i, carry):
        rows = pl.ds(pl.multiple_of(i * 128, 128), 128)
        turned = st_ref[rows, :].astype(jnp.float32).T
        xt[:, rows] = turned.astype(jnp.bfloat16)
        sq[pl.ds(i, 1), :] = jnp.sum(turned * turned, axis=0, keepdims=True)
        return carry

    token_live = lax.broadcasted_iota(jnp.int32, (1, TXT * GQ), 1) % TXT < len_ref[0]
    for load in loads[:4]:
        load.wait()
    score_scale = 1.0 / math.sqrt(HD)
    nt = (((1,), (1,)), ((), ()))
    for kh in range(KVH):
        cols = slice(kh * HD, (kh + 1) * HD)
        heads = [slice((kh * GQ + i) * HD, (kh * GQ + i + 1) * HD) for i in range(GQ)]
        query = jnp.concatenate([q_ref[:, h] for h in heads], axis=0)
        grad = jnp.concatenate([og_ref[:, h] for h in heads], axis=0)
        scores = lax.dot_general(k_ref[:, cols], query, nt, preferred_element_type=jnp.float32) * score_scale
        dprob = lax.dot_general(v_ref[:, cols], grad, nt, preferred_element_type=jnp.float32)
        dprob = jnp.where(token_live, dprob, 0.0)
        expo = jnp.exp(scores - jnp.max(scores, axis=0, keepdims=True))
        probs = expo * (1.0 / jnp.sum(expo, axis=0, keepdims=True))
        centre = jnp.sum(probs * dprob, axis=0, keepdims=True)
        dscore = (probs * (dprob - centre) * score_scale).astype(jnp.bfloat16)
        live_probs = jnp.where(token_live, probs, 0.0).astype(jnp.bfloat16)
        key_grad = jnp.dot(dscore, query, preferred_element_type=jnp.float32)
        value_grad = jnp.dot(live_probs, grad, preferred_element_type=jnp.float32)
        kv_ref[:, cols] = key_grad.astype(jnp.bfloat16)
        kv_ref[:, kh * HD + KVH * HD : (kh + 1) * HD + KVH * HD] = value_grad.astype(jnp.bfloat16)
    pl.semaphore_wait(barrier, len(peers))

    for name, half, dev in (("Zp0", 0, 1), ("Zm1", 1, 3), ("Zp1", 1, 1), ("Zm0", 0, 3)):
        send(name, own(half), block(0, 0, half), z_dev[dev])
    for name, half, dev in (("Xp00", 0, 1), ("Xm10", 1, 3), ("Xp10", 1, 1), ("Xm00", 0, 3)):
        send(name, own(half), block(0, 0, half), x_dev[dev])
    send("C00", kv_ref, block(0, 0, None), c_dev)
    g[rows_of(zh, x, c, None), :] = kv_ref[...]
    loads[4].wait()
    lax.fori_loop(0, ROWS // 128, squares, 0)
    for k in (1, 2, 3):
        send("Qx%d" % k, sq, sqx.at[k - 1], x_dev[k])
    for half in range(2):
        turned = jnp.broadcast_to(gn_ref[:, half * 128 : (half + 1) * 128], (128, 128)).T
        gn_col[half * 128 : (half + 1) * 128, :] = turned
    loads[5].wait()

    def x_send(zi, half):
        b = block(zi, 0, half)
        send("Xp%d%d" % (half, zi), b, b, x_dev[1])
        send("Xm%d%d" % (half, zi), b, b, x_dev[3])

    def core_send(zi, xi):
        b = block(zi, xi, None)
        send("C%d%d" % (zi, xi), b, b, c_dev)

    def x_near(zi):
        arrive("Xp0%d" % zi, block(zi, 1, 0))
        send("Gp0%d" % zi, block(zi, 1, 0), block(zi, 1, 0), x_dev[1])
        arrive("Xm1%d" % zi, block(zi, 2, 1))
        send("Gm1%d" % zi, block(zi, 2, 1), block(zi, 2, 1), x_dev[3])
        arrive("Xp1%d" % zi, block(zi, 1, 1))
        core_send(zi, 1)
        arrive("Xm0%d" % zi, block(zi, 2, 0))
        core_send(zi, 2)

    def x_far(zi):
        arrive("Gp0%d" % zi, block(zi, 3, 0))
        arrive("Gm1%d" % zi, block(zi, 3, 1))
        core_send(zi, 3)

    yo, yp, ym = up(y, 2), up(y, 1), up(y, -1)

    def level_rows(zi, base=0, size=512):
        return pl.ds(pl.multiple_of(zs[zi] * 512 + base, size), size)

    def part(zi, yy, half):
        return pl.ds(pl.multiple_of(zi * 512 + yy * SHARE + half * LAT, LAT), LAT)

    def slot(zi, half):
        return pl.ds(zi * SHARE + half * LAT, LAT)

    def terms(zi):
        for xi in range(4):
            arrive("C%d%d" % (zi, xi), g.at[rows_of(zs[zi], xs[xi], 1 - c, None)])
        made = lax.dot_general(
            g[level_rows(zi), :], w_ref[...], (((1,), (1,)), ((), ())), preferred_element_type=jnp.float32
        )
        rows = pl.ds(zi * 512, 512)
        tf[rows, :] = made
        tb[rows, :] = made.astype(jnp.bfloat16)
        send("Yo0%d" % zi, tb.at[part(zi, yo, 0)], ro.at[slot(zi, 0)], y_dev[1])
        send("Yo1%d" % zi, tb.at[part(zi, yo, 1)], ro.at[slot(zi, 1)], y_dev[3])
        send("Yn0%d" % zi, tb.at[part(zi, ym, 0)], rm.at[slot(zi, 0)], y_dev[3])
        send("Yn1%d" % zi, tb.at[part(zi, yp, 1)], rp.at[slot(zi, 1)], y_dev[1])

    def relay(zi):
        for half, to, into, dev in ((0, yp, rp, 1), (1, ym, rm, 3)):
            arrive("Yo%d%d" % (half, zi), ro.at[slot(zi, half)])
            total = tf[part(zi, to, half), :] + ro[slot(zi, half), :].astype(jnp.float32)
            sr[slot(zi, half), :] = total.astype(jnp.bfloat16)
            send("Yr%d%d" % (half, zi), sr.at[slot(zi, half)], into.at[slot(zi, half)], y_dev[dev])

    level_sends = []

    def settle(zi):
        for half, near, far in ((0, rm, rp), (1, rp, rm)):
            arrive("Yn%d%d" % (half, zi), near.at[slot(zi, half)])
            arrive("Yr%d%d" % (half, zi), far.at[slot(zi, half)])
        mine = pl.ds(pl.multiple_of(zi * 512 + y * SHARE, SHARE), SHARE)
        got = pl.ds(zi * SHARE, SHARE)
        total = tf[mine, :] + rp[got, :].astype(jnp.float32) + rm[got, :].astype(jnp.float32)
        k = up(zs[zi] - zl, 0)

        @pl.when(k == 0)
        def _():
            share_ref[...] = total

        made = pltpu.make_async_remote_copy(
            src_ref=sl.at[zi], dst_ref=rl.at[lax.max(k, 1) - 1],
            send_sem=send_sem.at[SLOT["L1"] + lax.max(k, 1) - 1],
            recv_sem=recv_sem.at[SLOT["L1"] + lax.max(k, 1) - 1],
            device_id=pipe_dev(zs[zi], y), device_id_type=pl.DeviceIdType.MESH,
        )

        @pl.when(k != 0)
        def _():
            sl[zi] = total.astype(jnp.bfloat16)
            made.start()

        level_sends.append((k, made))

    def weight_part(zi):
        def tile(i, carry):
            cols = pl.ds(pl.multiple_of(i * 256, 256), 256)
            made = jnp.dot(
                latt[:, level_rows(zi)], g[level_rows(zi), cols], preferred_element_type=jnp.float32
            )
            if zi == 0:
                wg_ref[:, cols] = made
            elif zi < 3:
                wg_ref[:, cols] = wg_ref[:, cols] + made
            else:
                wg_ref[:, cols] = (wg_ref[:, cols] + made) / GROUPS
            return carry

        lax.fori_loop(0, KVC // 256, tile, 0)

    def gain_part(zi, total):
        for j in range(4):
            rows = pl.ds(pl.multiple_of(zs[zi] * 512 + j * 128, 128), 128)
            scale = jnp.broadcast_to(inv[pl.ds(zs[zi] * 4 + j, 1), :], (128, 128)).T
            normed = st_ref[rows, :].astype(jnp.float32) * jnp.concatenate([scale, scale], axis=1)
            total = total + jnp.sum(tf[pl.ds(zi * 512 + j * 128, 128), :] * normed, axis=0, keepdims=True)
        return total

    def normalise(i, carry):
        rows = pl.ds(pl.multiple_of(i * 128, 128), 128)
        normed = xt[:, rows].astype(jnp.float32) * inv[pl.ds(i, 1), :]
        latt[:, rows] = (normed * gn_col[...]).astype(jnp.bfloat16)
        return carry

    x_near(0)
    x_far(0)
    for k in (1, 2, 3):
        arrive("Qx%d" % k, sqx.at[k - 1])
    sqs[0] = sq[...] + sqx[0] + sqx[1] + sqx[2]
    send("Qc", sqs.at[0], sqc, c_dev)
    terms(0)
    arrive("Qc", sqc)
    sqs[1] = sqs[0] + sqc[...]
    for k in (1, 2, 3):
        send("Qz%d" % k, sqs.at[1], sqz.at[k - 1], z_dev[k])
    arrive("Zp0", block(1, 0, 0))
    send("Fp0", block(1, 0, 0), block(1, 0, 0), z_dev[1])
    x_send(1, 0)
    arrive("Zm1", block(2, 0, 1))
    send("Fm1", block(2, 0, 1), block(2, 0, 1), z_dev[3])
    x_send(2, 1)
    relay(0)
    arrive("Zp1", block(1, 0, 1))
    x_send(1, 1)
    core_send(1, 0)
    arrive("Zm0", block(2, 0, 0))
    x_send(2, 0)
    core_send(2, 0)
    settle(0)
    x_near(1)
    x_near(2)
    arrive("Fp0", block(3, 0, 0))
    x_send(3, 0)
    arrive("Fm1", block(3, 0, 1))
    x_send(3, 1)
    core_send(3, 0)
    x_far(1)
    x_far(2)
    terms(1)
    terms(2)
    for k in (1, 2, 3):
        arrive("Qz%d" % k, sqz.at[k - 1])
    inv[...] = lax.rsqrt((sqs[1] + sqz[0] + sqz[1] + sqz[2]) / D + NORM_EPS)
    x_near(3)
    relay(1)
    relay(2)
    lax.fori_loop(0, ROWS // 128, normalise, 0)
    part_sum = gain_part(0, jnp.zeros((1, COLS), jnp.float32))
    weight_part(0)
    settle(1)
    settle(2)
    x_far(3)
    terms(3)
    for zi in (1, 2, 3):
        part_sum = gain_part(zi, part_sum)
    gs[...] = jnp.broadcast_to(part_sum, (8, COLS))
    for k in (1, 2, 3):
        send("Gy%d" % k, gs, gy.at[k - 1], y_dev[k])
    relay(3)
    weight_part(1)
    settle(3)
    for k in (1, 2, 3):
        arrive("Gy%d" % k, gy.at[k - 1])
    gs2[...] = gs[...] + gy[0] + gy[1] + gy[2]
    for k in (1, 2, 3):
        send("Gl%d" % k, gs2, gl.at[k - 1], l_dev[k])
    weight_part(2)
    weight_part(3)
    share = share_ref[...]
    for k in (1, 2, 3):
        arrive("L%d" % k, rl.at[k - 1])
        share = share + rl[k - 1].astype(jnp.float32)
    lat_ref[...] = share.astype(jnp.bfloat16)
    for k in (1, 2, 3):
        arrive("Gl%d" % k, gl.at[k - 1])
    gain_ref[...] = ((gs2[...] + gl[0] + gl[1] + gl[2]) / GROUPS)[0:1]
    for k, made in level_sends:
        @pl.when(k != 0)
        def _(made=made):
            made.wait_send()
    for made in started:
        made.wait_send()


def exchange(lengths, queries, out_grad, keys, values, weight, stream, gain):
    f32, bf16 = jnp.float32, jnp.bfloat16
    vmem = pl.BlockSpec(memory_space=pltpu.VMEM)
    count = len(SLOT)
    return pl.pallas_call(
        exchange_kernel,
        out_shape=(
            jax.ShapeDtypeStruct((COLS, KVC), f32),
            jax.ShapeDtypeStruct((SHARE, COLS), bf16),
            jax.ShapeDtypeStruct((1, COLS), f32),
        ),
        in_specs=[pl.BlockSpec(memory_space=pltpu.SMEM)] + [pl.BlockSpec(memory_space=pltpu.HBM)] * 6 + [vmem],
        out_specs=(vmem,) * 3,
        scratch_shapes=[
            pltpu.VMEM((TXT, HQ * HD), bf16),
            pltpu.VMEM((TXT, HQ * HD), bf16),
            pltpu.VMEM((LAT, KVH * HD), bf16),
            pltpu.VMEM((LAT, KVH * HD), bf16),
            pltpu.VMEM((COLS, KVC), bf16),
            pltpu.VMEM((ROWS, COLS), bf16),
            pltpu.VMEM((LAT, KVC), bf16),
            pltpu.VMEM((COLS, 128), f32),
            pltpu.SemaphoreType.DMA((6,)),
            pltpu.VMEM((ROWS, KVC), bf16),
            pltpu.VMEM((COLS, ROWS), bf16),
            pltpu.VMEM((COLS, ROWS), bf16),
            pltpu.VMEM((16, 128), f32),
            pltpu.VMEM((3, 16, 128), f32),
            pltpu.VMEM((3, 16, 128), f32),
            pltpu.VMEM((16, 128), f32),
            pltpu.VMEM((2, 16, 128), f32),
            pltpu.VMEM((16, 128), f32),
            pltpu.VMEM((ROWS, COLS), f32),
            pltpu.VMEM((ROWS, COLS), bf16),
            pltpu.VMEM((512, COLS), bf16),
            pltpu.VMEM((512, COLS), bf16),
            pltpu.VMEM((512, COLS), bf16),
            pltpu.VMEM((512, COLS), bf16),
            pltpu.VMEM((4, SHARE, COLS), bf16),
            pltpu.VMEM((3, SHARE, COLS), bf16),
            pltpu.VMEM((8, COLS), f32),
            pltpu.VMEM((3, 8, COLS), f32),
            pltpu.VMEM((8, COLS), f32),
            pltpu.VMEM((3, 8, COLS), f32),
            pltpu.VMEM((SHARE, COLS), f32),
            pltpu.SemaphoreType.DMA((count,)),
            pltpu.SemaphoreType.DMA((count,)),
        ],
        compiler_params=pltpu.CompilerParams(
            collective_id=0, has_side_effects=True, vmem_limit_bytes=56 * 1024 * 1024
        ),
        name="exchange",
    )(lengths, queries, out_grad, keys, values, weight, stream, gain)


def body(queries, out_grad, keys, values, kv_weight, stream, norm_gain, lengths):
    weight_grad, latent_grad, gain_grad = exchange(
        lengths, queries[0], out_grad[0], keys[0], values[0], kv_weight[0], stream, norm_gain.reshape(1, COLS)
    )
    return (weight_grad[None], latent_grad, gain_grad.reshape(COLS))


def solution(mesh):
    return jax.shard_map(
        body,
        mesh=mesh,
        in_specs=(
            P("pipe", "dp", None),
            P("pipe", "dp", None),
            P("pipe", "dp", None),
            P("pipe", "dp", None),
            P("pipe", "dp", None),
            P(None, "dp"),
            P("dp"),
            P("dp"),
        ),
        out_specs=(P("pipe", "dp", None), P("pipe", "dp"), P("dp")),
        check_vma=False,
    )
```

```python
import math

import jax
import jax.numpy as jnp
from jax import lax
from jax.experimental import pallas as pl
from jax.experimental.pallas import tpu as pltpu
from jax.sharding import PartitionSpec as P

D = 8192
HQ = 32
KVH = 4
HD = 128


NORM_EPS = 1e-05


ROWS = 2048
COLS = 256
KVC = 1024
LAT = 64
HALF = 32
PIPE = 16
GROUPS = 32
SHARE = 128
TXT = 128
GQ = HQ // KVH

GATHER = ["Zp0", "Zm1", "Zp1", "Zm0", "Fp0a", "Fm1a", "Fp0b", "Fm1b"]
GATHER += [n + str(i) for i in ("0", "1", "2", "3a", "3b") for n in ("Xp0", "Xm1", "Xp1", "Xm0", "Gp0", "Gm1")]
GATHER += ["C%d%d" % (i, j) for i in range(4) for j in range(4)]
OTHERS = ["Qz1", "Qz2", "Qz3", "Qx1", "Qx2", "Qx3", "Qc"]
OTHERS += [n + str(h) + str(i) for i in range(4) for h in range(2) for n in ("Yo", "Yn", "Yr")]
OTHERS += ["L1", "L2", "L3", "Gy1", "Gy2", "Gy3", "Gl1", "Gl2", "Gl3"]
SLOT = {n: i for i, n in enumerate(GATHER + OTHERS)}


def exchange_kernel(
    len_ref, q_hbm, og_hbm, k_hbm, v_hbm, w_hbm, st_hbm, gn_ref, wg_ref, lat_ref, gain_ref,
    q_ref, og_ref, k_ref, v_ref, w_ref, st_ref, kv_ref, gn_col, load_sem, g, xt, latt, sq, sqz, sqx, sqc, sqs, inv, tf, tb, ro, rp, rm, sr, sl, rl, gs, gy, gs2, gl, share_ref,
    send_sem, recv_sem,
):
    p = lax.axis_index("pipe")
    q = lax.axis_index("dp")
    zl, y = lax.div(p, 4), lax.rem(p, 4)
    zh, x, c = lax.div(q, 8), lax.rem(lax.div(q, 2), 4), lax.rem(q, 2)

    def up(a, k):
        return lax.rem(a + k + 4, 4)

    def dp_dev(zz, xx, cc):
        return (p, zz * 8 + xx * 2 + cc)

    def pipe_dev(zz, yy):
        return (zz * 4 + yy, q)

    z_dev = {k: dp_dev(up(zh, k), x, c) for k in (1, 3)}
    x_dev = {k: dp_dev(zh, up(x, k), c) for k in (1, 3)}
    c_dev = dp_dev(zh, x, 1 - c)
    y_dev = {k: pipe_dev(zl, up(y, k)) for k in (1, 3)}
    l_dev = {k: pipe_dev(up(zl, k), y) for k in (1, 2, 3)}
    peers = [*z_dev.values(), *x_dev.values(), c_dev, *y_dev.values(), *l_dev.values()]

    barrier = pltpu.get_barrier_semaphore()
    for peer in peers:
        pl.semaphore_signal(barrier, inc=1, device_id=peer, device_id_type=pl.DeviceIdType.MESH)

    loads = []
    pairs = ((q_hbm, q_ref), (k_hbm, k_ref), (og_hbm, og_ref), (v_hbm, v_ref), (st_hbm, st_ref), (w_hbm, w_ref))
    for n, (src, dst) in enumerate(pairs):
        load = pltpu.make_async_copy(src, dst, load_sem.at[n])
        load.start()
        loads.append(load)
    started = []

    def copy(name, src, dst, dev):
        s = SLOT[name]
        return pltpu.make_async_remote_copy(
            src_ref=src, dst_ref=dst, send_sem=send_sem.at[s], recv_sem=recv_sem.at[s],
            device_id=dev, device_id_type=pl.DeviceIdType.MESH,
        )

    def send(name, src, dst, dev):
        made = copy(name, src, dst, dev)
        made.start()
        started.append(made)

    def arrive(name, dst):
        copy(name, dst, dst, c_dev).wait_recv()

    def ring_send(name, src, into, devs):
        send(name + "1", src, into.at[0], devs[1])
        send(name + "3", src, into.at[2], devs[3])

    def ring_sum(name, src, into, devs):
        arrive(name + "1", into.at[0])
        send(name + "2", into.at[0], into.at[1], devs[1])
        arrive(name + "3", into.at[2])
        arrive(name + "2", into.at[1])
        return src[...] + into[0] + into[1] + into[2]

    def rows_of(zz, xx, cc, half, sub=None):
        start = ((zz * 4 + xx) * 2 + cc) * LAT
        if sub is not None:
            return pl.ds(pl.multiple_of(start + half * HALF + "ab".index(sub) * 16, 16), 16)
        if half is None:
            return pl.ds(pl.multiple_of(start, LAT), LAT)
        return pl.ds(pl.multiple_of(start + half * HALF, HALF), HALF)

    zs = [zh, up(zh, -1), up(zh, 1), up(zh, 2)]
    xs = [x, up(x, -1), up(x, 1), up(x, 2)]

    def block(zi, xi, half, sub=None):
        return g.at[rows_of(zs[zi], xs[xi], c, half, sub)]

    def own(half):
        return kv_ref.at[pl.ds(half * HALF, HALF)]

    def squares(i, carry):
        rows = pl.ds(pl.multiple_of(i * 128, 128), 128)
        turned = st_ref[rows, :].astype(jnp.float32).T
        xt[:, rows] = turned.astype(jnp.bfloat16)
        sq[pl.ds(i, 1), :] = jnp.sum(turned * turned, axis=0, keepdims=True)
        return carry

    token_live = lax.broadcasted_iota(jnp.int32, (1, TXT * GQ), 1) % TXT < len_ref[0]
    for load in loads[:4]:
        load.wait()
    score_scale = 1.0 / math.sqrt(HD)
    nt = (((1,), (1,)), ((), ()))
    for kh in range(KVH):
        cols = slice(kh * HD, (kh + 1) * HD)
        heads = [slice((kh * GQ + i) * HD, (kh * GQ + i + 1) * HD) for i in range(GQ)]
        query = jnp.concatenate([q_ref[:, h] for h in heads], axis=0)
        grad = jnp.concatenate([og_ref[:, h] for h in heads], axis=0)
        scores = lax.dot_general(k_ref[:, cols], query, nt, preferred_element_type=jnp.float32) * score_scale
        dprob = lax.dot_general(v_ref[:, cols], grad, nt, preferred_element_type=jnp.float32)
        dprob = jnp.where(token_live, dprob, 0.0)
        expo = jnp.exp(scores - jnp.max(scores, axis=0, keepdims=True))
        probs = expo * (1.0 / jnp.sum(expo, axis=0, keepdims=True))
        centre = jnp.sum(probs * dprob, axis=0, keepdims=True)
        dscore = (probs * (dprob - centre) * score_scale).astype(jnp.bfloat16)
        live_probs = jnp.where(token_live, probs, 0.0).astype(jnp.bfloat16)
        key_grad = jnp.dot(dscore, query, preferred_element_type=jnp.float32)
        value_grad = jnp.dot(live_probs, grad, preferred_element_type=jnp.float32)
        kv_ref[:, cols] = key_grad.astype(jnp.bfloat16)
        kv_ref[:, kh * HD + KVH * HD : (kh + 1) * HD + KVH * HD] = value_grad.astype(jnp.bfloat16)
    pl.semaphore_wait(barrier, len(peers))

    for name, half, dev in (("Zp0", 0, 1), ("Zm1", 1, 3), ("Zp1", 1, 1), ("Zm0", 0, 3)):
        send(name, own(half), block(0, 0, half), z_dev[dev])
    for name, half, dev in (("Xp00", 0, 1), ("Xm10", 1, 3), ("Xp10", 1, 1), ("Xm00", 0, 3)):
        send(name, own(half), block(0, 0, half), x_dev[dev])
    send("C00", kv_ref, block(0, 0, None), c_dev)
    g[rows_of(zh, x, c, None), :] = kv_ref[...]
    loads[4].wait()
    lax.fori_loop(0, ROWS // 128, squares, 0)
    ring_send("Qx", sq, sqx, x_dev)
    for half in range(2):
        turned = jnp.broadcast_to(gn_ref[:, half * 128 : (half + 1) * 128], (128, 128)).T
        gn_col[half * 128 : (half + 1) * 128, :] = turned
    loads[5].wait()

    def x_send(zi, half, sub=None):
        b = block(zi, 0, half, sub)
        tail = "%d%s" % (zi, sub or "")
        send("Xp%d%s" % (half, tail), b, b, x_dev[1])
        send("Xm%d%s" % (half, tail), b, b, x_dev[3])

    def core_send(zi, xi):
        b = block(zi, xi, None)
        send("C%d%d" % (zi, xi), b, b, c_dev)

    def x_near(zi, sub=None):
        tail = "%d%s" % (zi, sub or "")
        first, second = block(zi, 1, 0, sub), block(zi, 2, 1, sub)
        arrive("Xp0" + tail, first)
        send("Gp0" + tail, first, first, x_dev[1])
        arrive("Xm1" + tail, second)
        send("Gm1" + tail, second, second, x_dev[3])
        arrive("Xp1" + tail, block(zi, 1, 1, sub))
        if sub != "a":
            core_send(zi, 1)
        arrive("Xm0" + tail, block(zi, 2, 0, sub))
        if sub != "a":
            core_send(zi, 2)

    def x_far(zi, sub=None):
        tail = "%d%s" % (zi, sub or "")
        arrive("Gp0" + tail, block(zi, 3, 0, sub))
        arrive("Gm1" + tail, block(zi, 3, 1, sub))
        if sub != "a":
            core_send(zi, 3)

    yo, yp, ym = up(y, 2), up(y, 1), up(y, -1)

    def level_rows(zi, base=0, size=512):
        return pl.ds(pl.multiple_of(zs[zi] * 512 + base, size), size)

    def part(zi, yy, half):
        return pl.ds(pl.multiple_of(zi * 512 + yy * SHARE + half * LAT, LAT), LAT)

    def slot(zi, half):
        return pl.ds(zi * SHARE + half * LAT, LAT)

    def terms(zi):
        for xi in range(4):
            arrive("C%d%d" % (zi, xi), g.at[rows_of(zs[zi], xs[xi], 1 - c, None)])
        made = lax.dot_general(
            g[level_rows(zi), :], w_ref[...], (((1,), (1,)), ((), ())), preferred_element_type=jnp.float32
        )
        rows = pl.ds(zi * 512, 512)
        tf[rows, :] = made
        tb[rows, :] = made.astype(jnp.bfloat16)
        send("Yo0%d" % zi, tb.at[part(zi, yo, 0)], ro.at[slot(zi, 0)], y_dev[1])
        send("Yo1%d" % zi, tb.at[part(zi, yo, 1)], ro.at[slot(zi, 1)], y_dev[3])
        send("Yn0%d" % zi, tb.at[part(zi, ym, 0)], rm.at[slot(zi, 0)], y_dev[3])
        send("Yn1%d" % zi, tb.at[part(zi, yp, 1)], rp.at[slot(zi, 1)], y_dev[1])

    def relay(zi):
        for half, to, into, dev in ((0, yp, rp, 1), (1, ym, rm, 3)):
            arrive("Yo%d%d" % (half, zi), ro.at[slot(zi, half)])
            total = tf[part(zi, to, half), :] + ro[slot(zi, half), :].astype(jnp.float32)
            sr[slot(zi, half), :] = total.astype(jnp.bfloat16)
            send("Yr%d%d" % (half, zi), sr.at[slot(zi, half)], into.at[slot(zi, half)], y_dev[dev])

    level_sends = []

    def settle(zi):
        for half, near, far in ((0, rm, rp), (1, rp, rm)):
            arrive("Yn%d%d" % (half, zi), near.at[slot(zi, half)])
            arrive("Yr%d%d" % (half, zi), far.at[slot(zi, half)])
        mine = pl.ds(pl.multiple_of(zi * 512 + y * SHARE, SHARE), SHARE)
        got = pl.ds(zi * SHARE, SHARE)
        total = tf[mine, :] + rp[got, :].astype(jnp.float32) + rm[got, :].astype(jnp.float32)
        k = up(zs[zi] - zl, 0)

        @pl.when(k == 0)
        def _():
            share_ref[...] = total

        made = pltpu.make_async_remote_copy(
            src_ref=sl.at[zi], dst_ref=rl.at[lax.max(k, 1) - 1],
            send_sem=send_sem.at[SLOT["L1"] + lax.max(k, 1) - 1],
            recv_sem=recv_sem.at[SLOT["L1"] + lax.max(k, 1) - 1],
            device_id=pipe_dev(zs[zi], y), device_id_type=pl.DeviceIdType.MESH,
        )

        @pl.when(k != 0)
        def _():
            sl[zi] = total.astype(jnp.bfloat16)
            made.start()

        level_sends.append((k, made))

    def weight_part(zi):
        def tile(i, carry):
            cols = pl.ds(pl.multiple_of(i * 256, 256), 256)
            made = jnp.dot(
                latt[:, level_rows(zi)], g[level_rows(zi), cols], preferred_element_type=jnp.float32
            )
            if zi == 0:
                wg_ref[:, cols] = made
            elif zi < 3:
                wg_ref[:, cols] = wg_ref[:, cols] + made
            else:
                wg_ref[:, cols] = (wg_ref[:, cols] + made) / GROUPS
            return carry

        lax.fori_loop(0, KVC // 256, tile, 0)

    def gain_part(zi, total):
        for j in range(4):
            rows = pl.ds(pl.multiple_of(zs[zi] * 512 + j * 128, 128), 128)
            scale = jnp.broadcast_to(inv[pl.ds(zs[zi] * 4 + j, 1), :], (128, 128)).T
            normed = st_ref[rows, :].astype(jnp.float32) * jnp.concatenate([scale, scale], axis=1)
            total = total + jnp.sum(tf[pl.ds(zi * 512 + j * 128, 128), :] * normed, axis=0, keepdims=True)
        return total

    def normalise(i, carry):
        rows = pl.ds(pl.multiple_of(i * 128, 128), 128)
        normed = xt[:, rows].astype(jnp.float32) * inv[pl.ds(i, 1), :]
        latt[:, rows] = (normed * gn_col[...]).astype(jnp.bfloat16)
        return carry

    def far_z(sub):
        arrive("Fp0" + sub, block(3, 0, 0, sub))
        x_send(3, 0, sub)
        arrive("Fm1" + sub, block(3, 0, 1, sub))
        x_send(3, 1, sub)

    x_near(0)
    x_far(0)
    sqs[0] = ring_sum("Qx", sq, sqx, x_dev)
    send("Qc", sqs.at[0], sqc, c_dev)
    terms(0)
    arrive("Qc", sqc)
    sqs[1] = sqs[0] + sqc[...]
    ring_send("Qz", sqs.at[1], sqz, z_dev)
    arrive("Zp0", block(1, 0, 0))
    for sub in "ab":
        send("Fp0" + sub, block(1, 0, 0, sub), block(1, 0, 0, sub), z_dev[1])
    x_send(1, 0)
    arrive("Zm1", block(2, 0, 1))
    for sub in "ab":
        send("Fm1" + sub, block(2, 0, 1, sub), block(2, 0, 1, sub), z_dev[3])
    x_send(2, 1)
    relay(0)
    arrive("Zp1", block(1, 0, 1))
    x_send(1, 1)
    core_send(1, 0)
    arrive("Zm0", block(2, 0, 0))
    x_send(2, 0)
    core_send(2, 0)
    settle(0)
    x_near(1)
    x_near(2)
    far_z("a")
    x_far(1)
    far_z("b")
    core_send(3, 0)
    x_near(3, "a")
    x_far(2)
    terms(1)
    x_near(3, "b")
    terms(2)
    total_squares = ring_sum("Qz", sqs.at[1], sqz, z_dev)
    inv[...] = lax.rsqrt(total_squares / D + NORM_EPS)
    relay(1)
    x_far(3, "a")
    relay(2)
    part_sum = jnp.zeros((1, COLS), jnp.float32)
    for zi in range(3):
        part_sum = gain_part(zi, part_sum)
    x_far(3, "b")
    lax.fori_loop(0, ROWS // 128, normalise, 0)
    settle(1)
    terms(3)
    part_sum = gain_part(3, part_sum)
    gs[...] = jnp.broadcast_to(part_sum, (8, COLS))
    ring_send("Gy", gs, gy, y_dev)
    settle(2)
    weight_part(0)
    relay(3)
    weight_part(1)
    gs2[...] = ring_sum("Gy", gs, gy, y_dev)
    for k in (1, 2, 3):
        send("Gl%d" % k, gs2, gl.at[k - 1], l_dev[k])
    settle(3)
    weight_part(2)
    weight_part(3)
    share = share_ref[...]
    for k in (1, 2, 3):
        arrive("L%d" % k, rl.at[k - 1])
        share = share + rl[k - 1].astype(jnp.float32)
    lat_ref[...] = share.astype(jnp.bfloat16)
    for k in (1, 2, 3):
        arrive("Gl%d" % k, gl.at[k - 1])
    gain_ref[...] = ((gs2[...] + gl[0] + gl[1] + gl[2]) / GROUPS)[0:1]
    for k, made in level_sends:
        @pl.when(k != 0)
        def _(made=made):
            made.wait_send()
    for made in started:
        made.wait_send()


def exchange(lengths, queries, out_grad, keys, values, weight, stream, gain):
    f32, bf16 = jnp.float32, jnp.bfloat16
    vmem = pl.BlockSpec(memory_space=pltpu.VMEM)
    count = len(SLOT)
    return pl.pallas_call(
        exchange_kernel,
        out_shape=(
            jax.ShapeDtypeStruct((COLS, KVC), f32),
            jax.ShapeDtypeStruct((SHARE, COLS), bf16),
            jax.ShapeDtypeStruct((1, COLS), f32),
        ),
        in_specs=[pl.BlockSpec(memory_space=pltpu.SMEM)] + [pl.BlockSpec(memory_space=pltpu.HBM)] * 6 + [vmem],
        out_specs=(vmem,) * 3,
        scratch_shapes=[
            pltpu.VMEM((TXT, HQ * HD), bf16),
            pltpu.VMEM((TXT, HQ * HD), bf16),
            pltpu.VMEM((LAT, KVH * HD), bf16),
            pltpu.VMEM((LAT, KVH * HD), bf16),
            pltpu.VMEM((COLS, KVC), bf16),
            pltpu.VMEM((ROWS, COLS), bf16),
            pltpu.VMEM((LAT, KVC), bf16),
            pltpu.VMEM((COLS, 128), f32),
            pltpu.SemaphoreType.DMA((6,)),
            pltpu.VMEM((ROWS, KVC), bf16),
            pltpu.VMEM((COLS, ROWS), bf16),
            pltpu.VMEM((COLS, ROWS), bf16),
            pltpu.VMEM((16, 128), f32),
            pltpu.VMEM((3, 16, 128), f32),
            pltpu.VMEM((3, 16, 128), f32),
            pltpu.VMEM((16, 128), f32),
            pltpu.VMEM((2, 16, 128), f32),
            pltpu.VMEM((16, 128), f32),
            pltpu.VMEM((ROWS, COLS), f32),
            pltpu.VMEM((ROWS, COLS), bf16),
            pltpu.VMEM((512, COLS), bf16),
            pltpu.VMEM((512, COLS), bf16),
            pltpu.VMEM((512, COLS), bf16),
            pltpu.VMEM((512, COLS), bf16),
            pltpu.VMEM((4, SHARE, COLS), bf16),
            pltpu.VMEM((3, SHARE, COLS), bf16),
            pltpu.VMEM((8, COLS), f32),
            pltpu.VMEM((3, 8, COLS), f32),
            pltpu.VMEM((8, COLS), f32),
            pltpu.VMEM((3, 8, COLS), f32),
            pltpu.VMEM((SHARE, COLS), f32),
            pltpu.SemaphoreType.DMA((count,)),
            pltpu.SemaphoreType.DMA((count,)),
        ],
        compiler_params=pltpu.CompilerParams(
            collective_id=0, has_side_effects=True, vmem_limit_bytes=56 * 1024 * 1024
        ),
        name="exchange",
    )(lengths, queries, out_grad, keys, values, weight, stream, gain)


def body(queries, out_grad, keys, values, kv_weight, stream, norm_gain, lengths):
    weight_grad, latent_grad, gain_grad = exchange(
        lengths, queries[0], out_grad[0], keys[0], values[0], kv_weight[0], stream, norm_gain.reshape(1, COLS)
    )
    return (weight_grad[None], latent_grad, gain_grad.reshape(COLS))


def solution(mesh):
    return jax.shard_map(
        body,
        mesh=mesh,
        in_specs=(
            P("pipe", "dp", None),
            P("pipe", "dp", None),
            P("pipe", "dp", None),
            P("pipe", "dp", None),
            P("pipe", "dp", None),
            P(None, "dp"),
            P("dp"),
            P("dp"),
        ),
        out_specs=(P("pipe", "dp", None), P("pipe", "dp"), P("dp")),
        check_vma=False,
    )
```

```python
import math

import jax
import jax.numpy as jnp
from jax import lax
from jax.experimental import pallas as pl
from jax.experimental.pallas import tpu as pltpu
from jax.sharding import PartitionSpec as P

D = 8192
HQ = 32
KVH = 4
HD = 128


NORM_EPS = 1e-05


ROWS = 2048
COLS = 256
KVC = 1024
LAT = 64
HALF = 32
PIPE = 16
GROUPS = 32
SHARE = 128
TXT = 128
GQ = HQ // KVH

GATHER = ["Zp0", "Zm1", "Zp1", "Zm0", "Fp0a", "Fm1a", "Fp0b", "Fm1b"]
GATHER += [n + str(i) for i in ("0", "1", "2", "3a", "3b") for n in ("Xp0", "Xm1", "Xp1", "Xm0", "Gp0", "Gm1")]
GATHER += ["C%d%d" % (i, j) for i in range(4) for j in range(4)]
OTHERS = ["Qz1", "Qz2", "Qz3", "Qx1", "Qx2", "Qx3", "Qc"]
OTHERS += [n + str(h) + str(i) for i in range(4) for h in range(2) for n in ("Yo", "Yn", "Yr")]
OTHERS += ["L1", "L2", "L3", "Gy1", "Gy2", "Gy3", "Gl1", "Gl2", "Gl3"]
SLOT = {n: i for i, n in enumerate(GATHER + OTHERS)}


def exchange_kernel(
    len_ref, q_hbm, og_hbm, k_hbm, v_hbm, w_hbm, st_hbm, gn_ref, wg_ref, lat_ref, gain_ref,
    q_ref, og_ref, k_ref, v_ref, w_ref, st_ref, kv_ref, gn_col, load_sem, g, xt, latt, sq, sqz, sqx, sqc, sqs, inv, tf, tb, ro, rp, rm, sr, sl, rl, gs, gy, gs2, gl, share_ref,
    send_sem, recv_sem,
):
    p = lax.axis_index("pipe")
    q = lax.axis_index("dp")
    zl, y = lax.div(p, 4), lax.rem(p, 4)
    zh, x, c = lax.div(q, 8), lax.rem(lax.div(q, 2), 4), lax.rem(q, 2)

    def up(a, k):
        return lax.rem(a + k + 4, 4)

    def dp_dev(zz, xx, cc):
        return (p, zz * 8 + xx * 2 + cc)

    def pipe_dev(zz, yy):
        return (zz * 4 + yy, q)

    z_dev = {k: dp_dev(up(zh, k), x, c) for k in (1, 3)}
    x_dev = {k: dp_dev(zh, up(x, k), c) for k in (1, 3)}
    c_dev = dp_dev(zh, x, 1 - c)
    y_dev = {k: pipe_dev(zl, up(y, k)) for k in (1, 2, 3)}
    l_dev = {k: pipe_dev(up(zl, k), y) for k in (1, 2, 3)}
    peers = [*z_dev.values(), *x_dev.values(), c_dev, *y_dev.values(), *l_dev.values()]

    barrier = pltpu.get_barrier_semaphore()
    for peer in peers:
        pl.semaphore_signal(barrier, inc=1, device_id=peer, device_id_type=pl.DeviceIdType.MESH)

    loads = []
    pairs = ((q_hbm, q_ref), (k_hbm, k_ref), (og_hbm, og_ref), (v_hbm, v_ref), (st_hbm, st_ref), (w_hbm, w_ref))
    for n, (src, dst) in enumerate(pairs):
        load = pltpu.make_async_copy(src, dst, load_sem.at[n])
        load.start()
        loads.append(load)
    started = []

    def copy(name, src, dst, dev):
        s = SLOT[name]
        return pltpu.make_async_remote_copy(
            src_ref=src, dst_ref=dst, send_sem=send_sem.at[s], recv_sem=recv_sem.at[s],
            device_id=dev, device_id_type=pl.DeviceIdType.MESH,
        )

    def send(name, src, dst, dev):
        made = copy(name, src, dst, dev)
        made.start()
        started.append(made)

    def arrive(name, dst):
        copy(name, dst, dst, c_dev).wait_recv()

    def ring_send(name, src, into, devs):
        send(name + "1", src, into.at[0], devs[1])
        send(name + "3", src, into.at[2], devs[3])

    def ring_sum(name, src, into, devs):
        arrive(name + "1", into.at[0])
        send(name + "2", into.at[0], into.at[1], devs[1])
        arrive(name + "3", into.at[2])
        arrive(name + "2", into.at[1])
        return src[...] + into[0] + into[1] + into[2]

    def rows_of(zz, xx, cc, half, sub=None):
        start = ((zz * 4 + xx) * 2 + cc) * LAT
        if sub is not None:
            return pl.ds(pl.multiple_of(start + half * HALF + "ab".index(sub) * 16, 16), 16)
        if half is None:
            return pl.ds(pl.multiple_of(start, LAT), LAT)
        return pl.ds(pl.multiple_of(start + half * HALF, HALF), HALF)

    zs = [zh, up(zh, -1), up(zh, 1), up(zh, 2)]
    xs = [x, up(x, -1), up(x, 1), up(x, 2)]

    def block(zi, xi, half, sub=None):
        return g.at[rows_of(zs[zi], xs[xi], c, half, sub)]

    def own(half):
        return kv_ref.at[pl.ds(half * HALF, HALF)]

    def squares(i, carry):
        rows = pl.ds(pl.multiple_of(i * 128, 128), 128)
        turned = st_ref[rows, :].astype(jnp.float32).T
        xt[:, rows] = turned.astype(jnp.bfloat16)
        sq[pl.ds(i, 1), :] = jnp.sum(turned * turned, axis=0, keepdims=True)
        return carry

    token_live = lax.broadcasted_iota(jnp.int32, (1, TXT * GQ), 1) % TXT < len_ref[0]
    for load in loads[:4]:
        load.wait()
    score_scale = 1.0 / math.sqrt(HD)
    nt = (((1,), (1,)), ((), ()))
    for kh in range(KVH):
        cols = slice(kh * HD, (kh + 1) * HD)
        heads = [slice((kh * GQ + i) * HD, (kh * GQ + i + 1) * HD) for i in range(GQ)]
        query = jnp.concatenate([q_ref[:, h] for h in heads], axis=0)
        grad = jnp.concatenate([og_ref[:, h] for h in heads], axis=0)
        scores = lax.dot_general(k_ref[:, cols], query, nt, preferred_element_type=jnp.float32) * score_scale
        dprob = lax.dot_general(v_ref[:, cols], grad, nt, preferred_element_type=jnp.float32)
        dprob = jnp.where(token_live, dprob, 0.0)
        expo = jnp.exp(scores - jnp.max(scores, axis=0, keepdims=True))
        probs = expo * (1.0 / jnp.sum(expo, axis=0, keepdims=True))
        centre = jnp.sum(probs * dprob, axis=0, keepdims=True)
        dscore = (probs * (dprob - centre) * score_scale).astype(jnp.bfloat16)
        live_probs = jnp.where(token_live, probs, 0.0).astype(jnp.bfloat16)
        key_grad = jnp.dot(dscore, query, preferred_element_type=jnp.float32)
        value_grad = jnp.dot(live_probs, grad, preferred_element_type=jnp.float32)
        kv_ref[:, cols] = key_grad.astype(jnp.bfloat16)
        kv_ref[:, kh * HD + KVH * HD : (kh + 1) * HD + KVH * HD] = value_grad.astype(jnp.bfloat16)
    pl.semaphore_wait(barrier, len(peers))

    for name, half, dev in (("Zp0", 0, 1), ("Zm1", 1, 3), ("Zp1", 1, 1), ("Zm0", 0, 3)):
        send(name, own(half), block(0, 0, half), z_dev[dev])
    for name, half, dev in (("Xp00", 0, 1), ("Xm10", 1, 3), ("Xp10", 1, 1), ("Xm00", 0, 3)):
        send(name, own(half), block(0, 0, half), x_dev[dev])
    send("C00", kv_ref, block(0, 0, None), c_dev)
    g[rows_of(zh, x, c, None), :] = kv_ref[...]
    loads[4].wait()
    lax.fori_loop(0, ROWS // 128, squares, 0)
    ring_send("Qx", sq, sqx, x_dev)
    for half in range(2):
        turned = jnp.broadcast_to(gn_ref[:, half * 128 : (half + 1) * 128], (128, 128)).T
        gn_col[half * 128 : (half + 1) * 128, :] = turned
    loads[5].wait()

    def x_send(zi, half, sub=None):
        b = block(zi, 0, half, sub)
        tail = "%d%s" % (zi, sub or "")
        send("Xp%d%s" % (half, tail), b, b, x_dev[1])
        send("Xm%d%s" % (half, tail), b, b, x_dev[3])

    def core_send(zi, xi):
        b = block(zi, xi, None)
        send("C%d%d" % (zi, xi), b, b, c_dev)

    def x_near(zi, sub=None):
        tail = "%d%s" % (zi, sub or "")
        first, second = block(zi, 1, 0, sub), block(zi, 2, 1, sub)
        arrive("Xp0" + tail, first)
        send("Gp0" + tail, first, first, x_dev[1])
        arrive("Xm1" + tail, second)
        send("Gm1" + tail, second, second, x_dev[3])
        arrive("Xp1" + tail, block(zi, 1, 1, sub))
        if sub != "a":
            core_send(zi, 1)
        arrive("Xm0" + tail, block(zi, 2, 0, sub))
        if sub != "a":
            core_send(zi, 2)

    def x_far(zi, sub=None):
        tail = "%d%s" % (zi, sub or "")
        arrive("Gp0" + tail, block(zi, 3, 0, sub))
        arrive("Gm1" + tail, block(zi, 3, 1, sub))
        if sub != "a":
            core_send(zi, 3)

    yo, yp, ym = up(y, 2), up(y, 1), up(y, -1)

    def level_rows(zi, base=0, size=512):
        return pl.ds(pl.multiple_of(zs[zi] * 512 + base, size), size)

    def part(zi, yy, half):
        return pl.ds(pl.multiple_of(zi * 512 + yy * SHARE + half * LAT, LAT), LAT)

    def slot(zi, half):
        return pl.ds(zi * SHARE + half * LAT, LAT)

    def terms(zi):
        for xi in range(4):
            arrive("C%d%d" % (zi, xi), g.at[rows_of(zs[zi], xs[xi], 1 - c, None)])
        made = lax.dot_general(
            g[level_rows(zi), :], w_ref[...], (((1,), (1,)), ((), ())), preferred_element_type=jnp.float32
        )
        rows = pl.ds(zi * 512, 512)
        tf[rows, :] = made
        tb[rows, :] = made.astype(jnp.bfloat16)
        send("Yo0%d" % zi, tb.at[part(zi, yo, 0)], ro.at[slot(zi, 0)], y_dev[1])
        send("Yo1%d" % zi, tb.at[part(zi, yo, 1)], ro.at[slot(zi, 1)], y_dev[3])
        send("Yn0%d" % zi, tb.at[part(zi, ym, 0)], rm.at[slot(zi, 0)], y_dev[3])
        send("Yn1%d" % zi, tb.at[part(zi, yp, 1)], rp.at[slot(zi, 1)], y_dev[1])

    def relay(zi):
        for half, to, into, dev in ((0, yp, rp, 1), (1, ym, rm, 3)):
            arrive("Yo%d%d" % (half, zi), ro.at[slot(zi, half)])
            total = tf[part(zi, to, half), :] + ro[slot(zi, half), :].astype(jnp.float32)
            sr[slot(zi, half), :] = total.astype(jnp.bfloat16)
            send("Yr%d%d" % (half, zi), sr.at[slot(zi, half)], into.at[slot(zi, half)], y_dev[dev])

    level_sends = []

    def settle(zi):
        for half, near, far in ((0, rm, rp), (1, rp, rm)):
            arrive("Yn%d%d" % (half, zi), near.at[slot(zi, half)])
            arrive("Yr%d%d" % (half, zi), far.at[slot(zi, half)])
        mine = pl.ds(pl.multiple_of(zi * 512 + y * SHARE, SHARE), SHARE)
        got = pl.ds(zi * SHARE, SHARE)
        total = tf[mine, :] + rp[got, :].astype(jnp.float32) + rm[got, :].astype(jnp.float32)
        k = up(zs[zi] - zl, 0)

        @pl.when(k == 0)
        def _():
            share_ref[...] = total

        made = pltpu.make_async_remote_copy(
            src_ref=sl.at[zi], dst_ref=rl.at[lax.max(k, 1) - 1],
            send_sem=send_sem.at[SLOT["L1"] + lax.max(k, 1) - 1],
            recv_sem=recv_sem.at[SLOT["L1"] + lax.max(k, 1) - 1],
            device_id=pipe_dev(zs[zi], y), device_id_type=pl.DeviceIdType.MESH,
        )

        @pl.when(k != 0)
        def _():
            sl[zi] = total.astype(jnp.bfloat16)
            made.start()

        level_sends.append((k, made))

    def weight_part(zi):
        def tile(i, carry):
            cols = pl.ds(pl.multiple_of(i * 256, 256), 256)
            made = jnp.dot(
                latt[:, level_rows(zi)], g[level_rows(zi), cols], preferred_element_type=jnp.float32
            )
            if zi == 0:
                wg_ref[:, cols] = made
            elif zi < 3:
                wg_ref[:, cols] = wg_ref[:, cols] + made
            else:
                wg_ref[:, cols] = (wg_ref[:, cols] + made) / GROUPS
            return carry

        lax.fori_loop(0, KVC // 256, tile, 0)

    def gain_part(zi, total):
        for j in range(4):
            rows = pl.ds(pl.multiple_of(zs[zi] * 512 + j * 128, 128), 128)
            scale = jnp.broadcast_to(inv[pl.ds(zs[zi] * 4 + j, 1), :], (128, 128)).T
            normed = st_ref[rows, :].astype(jnp.float32) * jnp.concatenate([scale, scale], axis=1)
            total = total + jnp.sum(tf[pl.ds(zi * 512 + j * 128, 128), :] * normed, axis=0, keepdims=True)
        return total

    def normalise(i, carry):
        rows = pl.ds(pl.multiple_of(i * 128, 128), 128)
        normed = xt[:, rows].astype(jnp.float32) * inv[pl.ds(i, 1), :]
        latt[:, rows] = (normed * gn_col[...]).astype(jnp.bfloat16)
        return carry

    def far_z(sub):
        arrive("Fp0" + sub, block(3, 0, 0, sub))
        x_send(3, 0, sub)
        arrive("Fm1" + sub, block(3, 0, 1, sub))
        x_send(3, 1, sub)

    x_near(0)
    x_far(0)
    sqs[0] = ring_sum("Qx", sq, sqx, x_dev)
    send("Qc", sqs.at[0], sqc, c_dev)
    terms(0)
    arrive("Qc", sqc)
    sqs[1] = sqs[0] + sqc[...]
    ring_send("Qz", sqs.at[1], sqz, z_dev)
    arrive("Zp0", block(1, 0, 0))
    for sub in "ab":
        send("Fp0" + sub, block(1, 0, 0, sub), block(1, 0, 0, sub), z_dev[1])
    x_send(1, 0)
    arrive("Zm1", block(2, 0, 1))
    for sub in "ab":
        send("Fm1" + sub, block(2, 0, 1, sub), block(2, 0, 1, sub), z_dev[3])
    x_send(2, 1)
    relay(0)
    arrive("Zp1", block(1, 0, 1))
    x_send(1, 1)
    core_send(1, 0)
    arrive("Zm0", block(2, 0, 0))
    x_send(2, 0)
    core_send(2, 0)
    settle(0)
    x_near(1)
    x_near(2)
    far_z("a")
    x_far(1)
    far_z("b")
    core_send(3, 0)
    x_near(3, "a")
    x_far(2)
    terms(1)
    x_near(3, "b")
    terms(2)
    total_squares = ring_sum("Qz", sqs.at[1], sqz, z_dev)
    inv[...] = lax.rsqrt(total_squares / D + NORM_EPS)
    lax.fori_loop(0, ROWS // 128, normalise, 0)
    relay(1)
    x_far(3, "a")
    relay(2)
    weight_part(0)
    part_sum = jnp.zeros((1, COLS), jnp.float32)
    for zi in range(3):
        part_sum = gain_part(zi, part_sum)
    x_far(3, "b")
    settle(1)
    weight_part(1)
    terms(3)
    part_sum = gain_part(3, part_sum)
    gs[...] = jnp.broadcast_to(part_sum, (8, COLS))
    for k in (1, 2, 3):
        send("Gy%d" % k, gs, gy.at[k - 1], y_dev[k])
    settle(2)
    relay(3)
    weight_part(2)
    for k in (1, 2, 3):
        arrive("Gy%d" % k, gy.at[k - 1])
    gs2[...] = gs[...] + gy[0] + gy[1] + gy[2]
    for k in (1, 2, 3):
        send("Gl%d" % k, gs2, gl.at[k - 1], l_dev[k])
    settle(3)
    weight_part(3)
    share = share_ref[...]
    for k in (1, 2, 3):
        arrive("L%d" % k, rl.at[k - 1])
        share = share + rl[k - 1].astype(jnp.float32)
    lat_ref[...] = share.astype(jnp.bfloat16)
    for k in (1, 2, 3):
        arrive("Gl%d" % k, gl.at[k - 1])
    gain_ref[...] = ((gs2[...] + gl[0] + gl[1] + gl[2]) / GROUPS)[0:1]
    for k, made in level_sends:
        @pl.when(k != 0)
        def _(made=made):
            made.wait_send()
    for made in started:
        made.wait_send()


def exchange(lengths, queries, out_grad, keys, values, weight, stream, gain):
    f32, bf16 = jnp.float32, jnp.bfloat16
    vmem = pl.BlockSpec(memory_space=pltpu.VMEM)
    count = len(SLOT)
    return pl.pallas_call(
        exchange_kernel,
        out_shape=(
            jax.ShapeDtypeStruct((COLS, KVC), f32),
            jax.ShapeDtypeStruct((SHARE, COLS), bf16),
            jax.ShapeDtypeStruct((1, COLS), f32),
        ),
        in_specs=[pl.BlockSpec(memory_space=pltpu.SMEM)] + [pl.BlockSpec(memory_space=pltpu.HBM)] * 6 + [vmem],
        out_specs=(vmem,) * 3,
        scratch_shapes=[
            pltpu.VMEM((TXT, HQ * HD), bf16),
            pltpu.VMEM((TXT, HQ * HD), bf16),
            pltpu.VMEM((LAT, KVH * HD), bf16),
            pltpu.VMEM((LAT, KVH * HD), bf16),
            pltpu.VMEM((COLS, KVC), bf16),
            pltpu.VMEM((ROWS, COLS), bf16),
            pltpu.VMEM((LAT, KVC), bf16),
            pltpu.VMEM((COLS, 128), f32),
            pltpu.SemaphoreType.DMA((6,)),
            pltpu.VMEM((ROWS, KVC), bf16),
            pltpu.VMEM((COLS, ROWS), bf16),
            pltpu.VMEM((COLS, ROWS), bf16),
            pltpu.VMEM((16, 128), f32),
            pltpu.VMEM((3, 16, 128), f32),
            pltpu.VMEM((3, 16, 128), f32),
            pltpu.VMEM((16, 128), f32),
            pltpu.VMEM((2, 16, 128), f32),
            pltpu.VMEM((16, 128), f32),
            pltpu.VMEM((ROWS, COLS), f32),
            pltpu.VMEM((ROWS, COLS), bf16),
            pltpu.VMEM((512, COLS), bf16),
            pltpu.VMEM((512, COLS), bf16),
            pltpu.VMEM((512, COLS), bf16),
            pltpu.VMEM((512, COLS), bf16),
            pltpu.VMEM((4, SHARE, COLS), bf16),
            pltpu.VMEM((3, SHARE, COLS), bf16),
            pltpu.VMEM((8, COLS), f32),
            pltpu.VMEM((3, 8, COLS), f32),
            pltpu.VMEM((8, COLS), f32),
            pltpu.VMEM((3, 8, COLS), f32),
            pltpu.VMEM((SHARE, COLS), f32),
            pltpu.SemaphoreType.DMA((count,)),
            pltpu.SemaphoreType.DMA((count,)),
        ],
        compiler_params=pltpu.CompilerParams(
            collective_id=0, has_side_effects=True, vmem_limit_bytes=56 * 1024 * 1024
        ),
        name="exchange",
    )(lengths, queries, out_grad, keys, values, weight, stream, gain)


def body(queries, out_grad, keys, values, kv_weight, stream, norm_gain, lengths):
    weight_grad, latent_grad, gain_grad = exchange(
        lengths, queries[0], out_grad[0], keys[0], values[0], kv_weight[0], stream, norm_gain.reshape(1, COLS)
    )
    return (weight_grad[None], latent_grad, gain_grad.reshape(COLS))


def solution(mesh):
    return jax.shard_map(
        body,
        mesh=mesh,
        in_specs=(
            P("pipe", "dp", None),
            P("pipe", "dp", None),
            P("pipe", "dp", None),
            P("pipe", "dp", None),
            P("pipe", "dp", None),
            P(None, "dp"),
            P("dp"),
            P("dp"),
        ),
        out_specs=(P("pipe", "dp", None), P("pipe", "dp"), P("dp")),
        check_vma=False,
    )
```
